256 devices in a mesh: rows: 128 (over z, y, x), cols: 2 (over core).
Axes of the slice: x: 4, y: 4, z: 8, core: 2. Of those that a mesh axis runs over, the one named last changes fastest.
Arguments:
- design: float32 [131072, 512], P('rows', 'cols'), may hold values from -24 to 24
- signs: int32 [131072], P('rows'), may hold values from -1 to 1, as said below
- kept: int32 [8192], replicated, may hold values from 0 to 131071, as said below
Outputs:
- sketch: float32 [8192, 512], P('rows', 'cols')
- factor: float32 [512, 512], P(None, 'cols')
The draws below stay inside these ranges and needn't reach their ends.
Inputs may be any that keep to these rules, and one draw needn't show every extreme that they name: `signs`: each entry is +1 or -1. `kept`: distinct and increasing.
All inputs are finite; a program needn't handle non-finite values.
Results may differ from the reference program's by a relative error of at most 0.0003.
Values sent between devices are 32-bit elements; how exact they have to be, the bound alone decides.
No kernel may reach another device: no remote copies, remote signals or barrier semaphores. Data moves between devices by JAX's collectives and lax.ppermute only.
A program may use at most 64 MiB of HBM per device.

```python
import math
import jax
import jax.numpy as jnp
from jax import lax

P_SIZE = 512
ROWS_DEV = 1024
ROWS = 131072
KEPT = 8192
N_ROWS = 128


def draw_design(key, part):
    base = jax.random.fold_in(key, 11)
    first, second, third = jax.random.split(base, 3)
    column_scales = jnp.exp(jax.random.uniform(first, (P_SIZE,), jnp.float32, jnp.log(0.3), jnp.log(3.0)))
    noise = jax.random.normal(second, (ROWS, P_SIZE), jnp.float32)
    common = jax.random.normal(third, (ROWS, 1), jnp.float32)
    values = (noise + 0.6 * common) * column_scales[None, :]
    return jnp.clip(values, -24.0, 24.0).astype(jnp.float32)


def draw_signs(key, part):
    base = jax.random.fold_in(key, 22)
    return (2 * jax.random.randint(base, (ROWS,), 0, 2) - 1).astype(jnp.int32)


def draw_kept(key, part):
    base = jax.random.fold_in(key, 33)
    chosen = jax.random.permutation(base, ROWS)[:KEPT]
    return jnp.sort(chosen).astype(jnp.int32)


def setup_inputs(seed: int = 0) -> dict:
    arg_keys = jax.random.split(jax.random.key(seed), 4)
    design = draw_design(jax.random.fold_in(arg_keys[3], 71), 0)
    signs = draw_signs(jax.random.fold_in(arg_keys[3], 71), 0)
    kept = draw_kept(jax.random.fold_in(arg_keys[3], 71), 0)
    return dict(design=design, signs=signs, kept=kept)


def hadamard(order):
    matrix = jnp.ones((1, 1), jnp.float32)
    base = jnp.array([[1.0, 1.0], [1.0, -1.0]], jnp.float32)
    while matrix.shape[0] < order:
        matrix = jnp.kron(matrix, base)
    return matrix

def bit_parity(value):
    folded = value.astype(jnp.int32)
    for amount in (16, 8, 4, 2, 1):
        folded = jnp.bitwise_xor(folded, jnp.right_shift(folded, amount))
    return jnp.bitwise_and(folded, 1)

def local_transform(flipped):
    length, width = flipped.shape
    outer = length // 128
    inner_table = hadamard(128)
    outer_table = hadamard(outer)
    blocks = flipped.reshape(outer, 128, width)
    mixed = jnp.einsum('pb,abc->apc', inner_table, blocks, precision=lax.Precision.HIGHEST)
    mixed = jnp.einsum('qa,apc->qpc', outer_table, mixed, precision=lax.Precision.HIGHEST)
    return mixed.reshape(length, width)

def reference(design, signs, kept):
    length = ROWS_DEV
    kept_blocks = (kept // length).astype(jnp.int32)
    offsets = (kept - kept_blocks * length).astype(jnp.int32)
    scale = 1.0 / math.sqrt(ROWS)

    def step(total, block_row):
        start = (block_row * length).astype(jnp.int32)
        piece = lax.dynamic_slice_in_dim(design, start, length, 0)
        flips = lax.dynamic_slice_in_dim(signs, start, length, 0)
        transformed = local_transform(piece * flips.astype(jnp.float32)[:, None])
        parity = bit_parity(jnp.bitwise_and(kept_blocks, block_row))
        factor = (1.0 - 2.0 * parity.astype(jnp.float32)) * scale
        return (total + jnp.take(transformed, offsets, axis=0) * factor[:, None], None)
    start_total = jnp.zeros((KEPT, P_SIZE), jnp.float32)
    sketch, unused = lax.scan(step, start_total, jnp.arange(N_ROWS, dtype=jnp.int32))
    gram = jnp.dot(sketch.T.astype(jnp.float32), sketch.astype(jnp.float32), precision=lax.Precision.HIGHEST, preferred_element_type=jnp.float32) / KEPT
    factor = jnp.linalg.cholesky(gram).T
    return (sketch, factor)
```

```python
import functools
import math

import jax
import jax.numpy as jnp
from jax import lax
from jax.experimental import pallas as pl
from jax.experimental.pallas import tpu as pltpu
from jax.sharding import Mesh
from jax.sharding import PartitionSpec as P

ROWS = ("rows_0", "rows_1", "rows_2")
PLANE = ("rows_1", "rows_2")
VMEM = pl.BlockSpec(memory_space=pltpu.VMEM)
SMEM = pl.BlockSpec(memory_space=pltpu.SMEM)
LIMIT = pltpu.CompilerParams(vmem_limit_bytes=32 * 1024 * 1024)
WINDOW = 4


def butterflies(values):
    values = list(values)
    half = 1
    while half < len(values):
        for low in range(len(values)):
            if not low & half:
                a, b = values[low], values[low | half]
                values[low], values[low | half] = a + b, a - b
        half *= 2
    return values


def sylvester(order):
    parity = lax.broadcasted_iota(jnp.int32, (order, order), 0)
    parity = parity & lax.broadcasted_iota(jnp.int32, (order, order), 1)
    for amount in (4, 2, 1):
        parity = parity ^ (parity >> amount)
    return (1 - 2 * (parity & 1)).astype(jnp.float32).astype(jnp.bfloat16)


def local_kernel(design_ref, signs_ref, out_ref):
    table = sylvester(128)
    for half in range(2):
        parts = []
        for b in range(8):
            piece = design_ref[b * 128 : (b + 1) * 128, half * 128 : (half + 1) * 128].T
            piece = piece * signs_ref[b : b + 1, :].astype(jnp.float32)
            high = piece.astype(jnp.bfloat16)
            rest = piece - high.astype(jnp.float32)
            middle = rest.astype(jnp.bfloat16)
            low = (rest - middle.astype(jnp.float32)).astype(jnp.bfloat16)
            total = jnp.dot(low, table, preferred_element_type=jnp.float32)
            total += jnp.dot(middle, table, preferred_element_type=jnp.float32)
            total += jnp.dot(high, table, preferred_element_type=jnp.float32)
            parts.append(total)
        for q, mixed in enumerate(butterflies(parts)):
            out_ref[pl.ds(half * 8 + q, 128, stride=16), :] = mixed


def select_kernel(scale, columns_ref, kept_ref, kept_scalar_ref, out_ref, work, first, second):
    for low in range(16):
        mixed = butterflies(columns_ref[high * 16 + low] for high in range(8))
        for high in range(8):
            work[high * 16 + low] = mixed[high]
    for high in range(8):
        mixed = butterflies(work[high * 16 + low] for low in range(16))
        for low in range(16):
            work[high * 16 + low] = mixed[low]
    sublane = lax.broadcasted_iota(jnp.int32, (8, 128), 0)

    def picked(block, lane, key, so_far):
        found = key == sublane + block * 8
        return tuple(
            jnp.where(found, jnp.take_along_axis(work[block, h * 8 : h * 8 + 8, :], lane, axis=1), so_far[h])
            for h in range(2)
        )

    def ids(chunk):
        wanted = jnp.broadcast_to(kept_ref[pl.ds(chunk, 1), :], (8, 128))
        return wanted & 127, wanted >> 7

    zero = jnp.zeros((8, 128), jnp.float32)

    def group(step, carry):
        for inner in range(8):
            chunk = step * 8 + inner
            start = kept_scalar_ref[chunk * 128] >> 10
            lane, key = ids(chunk)
            so_far = (zero, zero)
            for w in range(WINDOW):
                so_far = picked(jnp.minimum(start + w, 127), lane, key, so_far)
            first[pl.ds(chunk, 1), :] = jnp.sum(so_far[0], axis=0, keepdims=True)
            second[pl.ds(chunk, 1), :] = jnp.sum(so_far[1], axis=0, keepdims=True)
        return carry

    lax.fori_loop(0, 8, group, 0)

    def rest(chunk, carry):
        start = (kept_scalar_ref[chunk * 128] >> 10) + WINDOW
        stop = (kept_scalar_ref[chunk * 128 + 127] >> 10) + 1

        @pl.when(stop > start)
        def _():
            lane, key = ids(chunk)
            more = lax.fori_loop(start, stop, lambda block, c: picked(block, lane, key, c), (zero, zero))
            first[pl.ds(chunk, 1), :] += jnp.sum(more[0], axis=0, keepdims=True)
            second[pl.ds(chunk, 1), :] += jnp.sum(more[1], axis=0, keepdims=True)

        return carry

    lax.fori_loop(0, 64, rest, 0)
    left = lax.broadcasted_iota(jnp.int32, (64, 128), 1) < 64
    a, b = first[...] * scale, second[...] * scale
    out_ref[pl.ds(0, 64, stride=2), :] = jnp.where(left, a, pltpu.roll(b, 64, 1))
    out_ref[pl.ds(1, 64, stride=2), :] = jnp.where(left, pltpu.roll(a, 64, 1), b)


def turn_kernel(entries_ref, sketch_ref):
    turned = entries_ref[...].T
    sketch_ref[:, :128] = turned[:64]
    sketch_ref[:, 128:] = turned[64:]


def gram_kernel(scale, column_ref, own_ref, other_ref, out_ref):
    own = [own_ref[:, :128], own_ref[:, 128:]]
    other = [other_ref[:, :128], other_ref[:, 128:]]
    zero = column_ref[0] == 0

    def choose(a, b):
        return jnp.where(zero, a, b)

    left = choose(own[0], other[1])
    pairs = [
        (own[0], own[0]),
        (own[0], own[1]),
        (own[1], own[1]),
        (left, choose(other[0], own[0])),
        (left, choose(other[1], own[1])),
    ]
    for index, (a, b) in enumerate(pairs):
        out_ref[index * 128 : (index + 1) * 128, :] = scale * lax.dot_general(
            a, b, (((0,), (0,)), ((), ())), precision=lax.Precision.HIGHEST, preferred_element_type=jnp.float32
        )


def copies(shard, axes, count):
    return lax.all_to_all(jnp.broadcast_to(shard[None], (count, *shard.shape)), axes, 0, 0, tiled=True)


def swap_cores(value):
    return lax.ppermute(value, "cols", [(0, 1), (1, 0)])


def whole_gram(first, second):
    b = [first[i * 128 : (i + 1) * 128] for i in range(5)]
    d = [second[i * 128 : (i + 1) * 128] for i in range(5)]
    rows = [
        [b[0], b[1], b[3], b[4]],
        [b[1].T, b[2], d[3], d[4]],
        [b[3].T, d[3].T, d[0], d[1]],
        [b[4].T, d[4].T, d[1].T, d[2]],
    ]
    return jnp.concatenate([jnp.concatenate(r, 1) for r in rows], 0)


def body(design, signs, kept):
    f32 = jnp.float32
    column = lax.axis_index("cols")
    local = pl.pallas_call(
        local_kernel,
        out_shape=jax.ShapeDtypeStruct((2048, 128), f32),
        in_specs=[VMEM, VMEM],
        out_specs=VMEM,
        compiler_params=LIMIT,
        name="local_transform",
    )(design, signs.reshape(8, 128))
    columns = lax.all_to_all(local.reshape(128, 16, 128), ROWS, 0, 0, tiled=True)
    entries = pl.pallas_call(
        functools.partial(select_kernel, 1.0 / math.sqrt(131072)),
        out_shape=jax.ShapeDtypeStruct((128, 128), f32),
        in_specs=[VMEM, VMEM, SMEM],
        out_specs=VMEM,
        scratch_shapes=[
            pltpu.VMEM((128, 16, 128), f32),
            pltpu.VMEM((64, 128), f32),
            pltpu.VMEM((64, 128), f32),
        ],
        compiler_params=LIMIT,
        name="select",
    )(columns, kept.reshape(64, 128), kept)
    entries = lax.all_to_all(entries.reshape(128, 1, 128), ROWS, 0, 0, tiled=True)
    sketch = pl.pallas_call(
        turn_kernel,
        out_shape=jax.ShapeDtypeStruct((64, 256), f32),
        in_specs=[VMEM],
        out_specs=VMEM,
        name="turn",
    )(entries.reshape(128, 128))
    other = swap_cores(sketch)
    partial = pl.pallas_call(
        functools.partial(gram_kernel, 1.0 / 8192),
        out_shape=jax.ShapeDtypeStruct((640, 128), f32),
        in_specs=[SMEM, VMEM, VMEM],
        out_specs=VMEM,
        compiler_params=LIMIT,
        name="gram",
    )(column.reshape(1), sketch, other)
    share = jnp.sum(lax.all_to_all(partial.reshape(16, 40, 128), PLANE, 0, 0, tiled=True), axis=0)
    share = jnp.sum(copies(share, "rows_0", 8), axis=0)
    mine = copies(share, PLANE, 16).reshape(640, 128)
    theirs = swap_cores(mine)
    first = jnp.where(column == 0, mine, theirs)
    second = jnp.where(column == 0, theirs, mine)
    factor = jnp.linalg.cholesky(whole_gram(first, second)).T
    return sketch, lax.dynamic_slice_in_dim(factor, column * 256, 256, 1)


def solution(mesh):
    torus = Mesh(
        mesh.devices.reshape(8, 4, 4, mesh.shape["cols"]), ("rows_0", "rows_1", "rows_2", "cols")
    )
    return jax.shard_map(
        body,
        mesh=torus,
        in_specs=(P(ROWS, "cols"), P(ROWS), P()),
        out_specs=(P(ROWS, "cols"), P(None, "cols")),
        check_vma=False,
    )
```

```python
import functools
import math

import jax
import jax.numpy as jnp
from jax import lax
from jax.experimental import pallas as pl
from jax.experimental.pallas import tpu as pltpu
from jax.sharding import Mesh
from jax.sharding import PartitionSpec as P

ROWS = ("rows_0", "rows_1", "rows_2")
PLANE = ("rows_1", "rows_2")
VMEM = pl.BlockSpec(memory_space=pltpu.VMEM)
SMEM = pl.BlockSpec(memory_space=pltpu.SMEM)
LIMIT = pltpu.CompilerParams(vmem_limit_bytes=32 * 1024 * 1024)
WINDOW = 4


def butterflies(values):
    values = list(values)
    half = 1
    while half < len(values):
        for low in range(len(values)):
            if not low & half:
                a, b = values[low], values[low | half]
                values[low], values[low | half] = a + b, a - b
        half *= 2
    return values


def sylvester(order):
    parity = lax.broadcasted_iota(jnp.int32, (order, order), 0)
    parity = parity & lax.broadcasted_iota(jnp.int32, (order, order), 1)
    for amount in (4, 2, 1):
        parity = parity ^ (parity >> amount)
    return (1 - 2 * (parity & 1)).astype(jnp.float32).astype(jnp.bfloat16)


def local_kernel(design_ref, signs_ref, out_ref):
    table = sylvester(128)
    for half in range(2):
        parts = []
        for b in range(8):
            piece = design_ref[b * 128 : (b + 1) * 128, half * 128 : (half + 1) * 128].T
            piece = piece * signs_ref[b : b + 1, :].astype(jnp.float32)
            high = piece.astype(jnp.bfloat16)
            rest = piece - high.astype(jnp.float32)
            middle = rest.astype(jnp.bfloat16)
            low = (rest - middle.astype(jnp.float32)).astype(jnp.bfloat16)
            total = jnp.dot(low, table, preferred_element_type=jnp.float32)
            total += jnp.dot(middle, table, preferred_element_type=jnp.float32)
            total += jnp.dot(high, table, preferred_element_type=jnp.float32)
            parts.append(total)
        for q, mixed in enumerate(butterflies(parts)):
            out_ref[pl.ds(half * 8 + q, 128, stride=16), :] = mixed


def select_kernel(scale, columns_ref, kept_ref, kept_scalar_ref, out_ref, work, first, second):
    for low in range(16):
        mixed = butterflies(columns_ref[high * 16 + low] for high in range(8))
        for high in range(8):
            work[high * 16 + low] = mixed[high]
    for high in range(8):
        mixed = butterflies(work[high * 16 + low] for low in range(16))
        for low in range(16):
            work[high * 16 + low] = mixed[low]
    sublane = lax.broadcasted_iota(jnp.int32, (8, 128), 0)

    def picked(block, lane, key, so_far):
        found = key == sublane + block * 8
        return tuple(
            jnp.where(found, jnp.take_along_axis(work[block, h * 8 : h * 8 + 8, :], lane, axis=1), so_far[h])
            for h in range(2)
        )

    def ids(chunk):
        wanted = jnp.broadcast_to(kept_ref[pl.ds(chunk, 1), :], (8, 128))
        return wanted & 127, wanted >> 7

    zero = jnp.zeros((8, 128), jnp.float32)

    def group(step, carry):
        for inner in range(8):
            chunk = step * 8 + inner
            start = kept_scalar_ref[chunk * 128] >> 10
            lane, key = ids(chunk)
            so_far = (zero, zero)
            for w in range(WINDOW):
                so_far = picked(jnp.minimum(start + w, 127), lane, key, so_far)
            first[pl.ds(chunk, 1), :] = jnp.sum(so_far[0], axis=0, keepdims=True)
            second[pl.ds(chunk, 1), :] = jnp.sum(so_far[1], axis=0, keepdims=True)
        return carry

    lax.fori_loop(0, 8, group, 0)

    def rest(chunk, carry):
        start = (kept_scalar_ref[chunk * 128] >> 10) + WINDOW
        stop = (kept_scalar_ref[chunk * 128 + 127] >> 10) + 1

        @pl.when(stop > start)
        def _():
            lane, key = ids(chunk)
            more = lax.fori_loop(start, stop, lambda block, c: picked(block, lane, key, c), (zero, zero))
            first[pl.ds(chunk, 1), :] += jnp.sum(more[0], axis=0, keepdims=True)
            second[pl.ds(chunk, 1), :] += jnp.sum(more[1], axis=0, keepdims=True)

        return carry

    lax.fori_loop(0, 64, rest, 0)
    left = lax.broadcasted_iota(jnp.int32, (64, 128), 1) < 64
    a, b = first[...] * scale, second[...] * scale
    out_ref[pl.ds(0, 64, stride=2), :] = jnp.where(left, a, pltpu.roll(b, 64, 1))
    out_ref[pl.ds(1, 64, stride=2), :] = jnp.where(left, pltpu.roll(a, 64, 1), b)


def turn_kernel(entries_ref, sketch_ref):
    turned = entries_ref[...].T
    sketch_ref[:, :128] = turned[:64]
    sketch_ref[:, 128:] = turned[64:]


def gram_kernel(scale, column_ref, own_ref, other_ref, out_ref):
    own = [own_ref[:, :128], own_ref[:, 128:]]
    other = [other_ref[:, :128], other_ref[:, 128:]]
    zero = column_ref[0] == 0

    def choose(a, b):
        return jnp.where(zero, a, b)

    left = choose(own[0], other[1])
    pairs = [
        (own[0], own[0]),
        (own[0], own[1]),
        (own[1], own[1]),
        (left, choose(other[0], own[0])),
        (left, choose(other[1], own[1])),
    ]
    for index, (a, b) in enumerate(pairs):
        out_ref[index * 128 : (index + 1) * 128, :] = scale * lax.dot_general(
            a, b, (((0,), (0,)), ((), ())), precision=lax.Precision.HIGHEST, preferred_element_type=jnp.float32
        )


def copies(shard, axes, count):
    return lax.all_to_all(jnp.broadcast_to(shard[None], (count, *shard.shape)), axes, 0, 0, tiled=True)


def swap_cores(value):
    return lax.ppermute(value, "cols", [(0, 1), (1, 0)])


def high_dot(a, b, dims):
    return lax.dot_general(a, b, (dims, ((), ())), precision=lax.Precision.HIGHEST, preferred_element_type=jnp.float32)


def spread(row):
    return jnp.broadcast_to(row, (8, 128))


def factor_block(block, upper_ref, inverse_ref):
    lanes = lax.broadcasted_iota(jnp.int32, (8, 128), 1)
    strips = [block[8 * s : 8 * s + 8] for s in range(16)]
    for s in range(16):
        here = strips[s]
        base = 8 * s
        inside = (lanes >= base) & (lanes < base + 8)
        columns = [spread(here[:, base + k : base + k + 1]) for k in range(8)]
        e = [[spread(columns[k][i : i + 1]) if k >= i else None for k in range(8)] for i in range(8)]
        m = [jnp.where(inside, jnp.where(lanes == base + k, 1.0, 0.0), spread(here[k : k + 1])) for k in range(8)]
        d, u, r = [None] * 8, [[None] * 8 for _ in range(8)], [None] * 8
        for k in range(8):
            d[k] = lax.rsqrt(e[k][k])
            for j in range(k + 1, 8):
                u[k][j] = e[k][j] * d[k]
            r[k] = m[k] * d[k]
            for i in range(k + 1, 8):
                for j in range(i, 8):
                    e[i][j] = e[i][j] - u[k][i] * u[k][j]
            for i in range(k + 1, 8):
                m[i] = m[i] - u[k][i] * r[k]
        z = [None] * 8
        for k in reversed(range(8)):
            z[k] = r[k] * d[k]
            for j in reversed(range(k + 1, 8)):
                z[k] = z[k] - (u[k][j] * d[k]) * z[j]
        for t in range(s + 1, 16):
            there = strips[t]
            total = jnp.where(inside, 0.0, there)
            for k in range(8):
                total = total - spread(there[:, base + k : base + k + 1]) * z[k]
            strips[t] = total
        for k in range(8):
            row = r[k]
            inverse_ref[base + k : base + k + 1, :] = jnp.where(lanes < base + 8, row, 0.0)[:1]
            row = jnp.where(lanes < base + 8, 0.0, row)
            row = jnp.where(lanes == base + k, e[k][k] * d[k], row)
            for j in range(k + 1, 8):
                row = jnp.where(lanes == base + j, u[k][j], row)
            upper_ref[base + k : base + k + 1, :] = row[:1]


def cholesky_kernel(column_ref, mine_ref, theirs_ref, out_ref, gram, upper, inverse):
    zero = column_ref[0] == 0
    names = [(0, 0), (0, 1), (1, 1), (0, 2), (0, 3), (2, 2), (2, 3), (3, 3), (1, 2), (1, 3)]
    place = {name: i for i, name in enumerate(names)}
    a = {}
    for i in range(5):
        x, y = mine_ref[i * 128 : i * 128 + 128, :], theirs_ref[i * 128 : i * 128 + 128, :]
        a[names[i]] = jnp.where(zero, x, y)
        a[names[5 + i]] = jnp.where(zero, y, x)
    for name in names:
        gram[place[name]] = a[name]
    for p in range(4):
        factor_block(gram[place[p, p]], upper.at[p * 4 + p], inverse)
        for q in range(p + 1, 4):
            upper[p * 4 + q] = high_dot(inverse[...], gram[place[p, q]], ((1,), (0,)))
        for i in range(p + 1, 4):
            for j in range(i, 4):
                gram[place[i, j]] = gram[place[i, j]] - high_dot(upper[p * 4 + i], upper[p * 4 + j], ((0,), (0,)))
        for q in range(p):
            upper[p * 4 + q] = jnp.zeros((128, 128), jnp.float32)
    for p in range(4):
        for h in range(2):
            out_ref[p * 128 : p * 128 + 128, h * 128 : h * 128 + 128] = jnp.where(zero, upper[p * 4 + h], upper[p * 4 + 2 + h])


def body(design, signs, kept):
    f32 = jnp.float32
    column = lax.axis_index("cols")
    local = pl.pallas_call(
        local_kernel,
        out_shape=jax.ShapeDtypeStruct((2048, 128), f32),
        in_specs=[VMEM, VMEM],
        out_specs=VMEM,
        compiler_params=LIMIT,
        name="local_transform",
    )(design, signs.reshape(8, 128))
    columns = lax.all_to_all(local.reshape(128, 16, 128), ROWS, 0, 0, tiled=True)
    entries = pl.pallas_call(
        functools.partial(select_kernel, 1.0 / math.sqrt(131072)),
        out_shape=jax.ShapeDtypeStruct((128, 128), f32),
        in_specs=[VMEM, VMEM, SMEM],
        out_specs=VMEM,
        scratch_shapes=[
            pltpu.VMEM((128, 16, 128), f32),
            pltpu.VMEM((64, 128), f32),
            pltpu.VMEM((64, 128), f32),
        ],
        compiler_params=LIMIT,
        name="select",
    )(columns, kept.reshape(64, 128), kept)
    entries = lax.all_to_all(entries.reshape(128, 1, 128), ROWS, 0, 0, tiled=True)
    sketch = pl.pallas_call(
        turn_kernel,
        out_shape=jax.ShapeDtypeStruct((64, 256), f32),
        in_specs=[VMEM],
        out_specs=VMEM,
        name="turn",
    )(entries.reshape(128, 128))
    other = swap_cores(sketch)
    partial = pl.pallas_call(
        functools.partial(gram_kernel, 1.0 / 8192),
        out_shape=jax.ShapeDtypeStruct((640, 128), f32),
        in_specs=[SMEM, VMEM, VMEM],
        out_specs=VMEM,
        compiler_params=LIMIT,
        name="gram",
    )(column.reshape(1), sketch, other)
    share = jnp.sum(lax.all_to_all(partial.reshape(16, 40, 128), PLANE, 0, 0, tiled=True), axis=0)
    share = jnp.sum(copies(share, "rows_0", 8), axis=0)
    mine = copies(share, PLANE, 16).reshape(640, 128)
    theirs = swap_cores(mine)
    factor = pl.pallas_call(
        cholesky_kernel,
        out_shape=jax.ShapeDtypeStruct((512, 256), f32),
        in_specs=[SMEM, VMEM, VMEM],
        out_specs=VMEM,
        scratch_shapes=[
            pltpu.VMEM((10, 128, 128), f32),
            pltpu.VMEM((16, 128, 128), f32),
            pltpu.VMEM((128, 128), f32),
        ],
        compiler_params=LIMIT,
        name="cholesky",
    )(column.reshape(1), mine, theirs)
    return sketch, factor


def solution(mesh):
    torus = Mesh(
        mesh.devices.reshape(8, 4, 4, mesh.shape["cols"]), ("rows_0", "rows_1", "rows_2", "cols")
    )
    return jax.shard_map(
        body,
        mesh=torus,
        in_specs=(P(ROWS, "cols"), P(ROWS), P()),
        out_specs=(P(ROWS, "cols"), P(None, "cols")),
        check_vma=False,
    )
```

```python
import functools
import math

import jax
import jax.numpy as jnp
from jax import lax
from jax.experimental import pallas as pl
from jax.experimental.pallas import tpu as pltpu
from jax.sharding import Mesh
from jax.sharding import PartitionSpec as P

ROWS = ("rows_0", "rows_1", "rows_2")
PLANE = ("rows_1", "rows_2")
VMEM = pl.BlockSpec(memory_space=pltpu.VMEM)
SMEM = pl.BlockSpec(memory_space=pltpu.SMEM)
LIMIT = pltpu.CompilerParams(vmem_limit_bytes=32 * 1024 * 1024)
WINDOW = 4
GROUP = 1
AHEAD = 2


def butterflies(values):
    values = list(values)
    half = 1
    while half < len(values):
        for low in range(len(values)):
            if not low & half:
                a, b = values[low], values[low | half]
                values[low], values[low | half] = a + b, a - b
        half *= 2
    return values


def sylvester(order):
    parity = lax.broadcasted_iota(jnp.int32, (order, order), 0)
    parity = parity & lax.broadcasted_iota(jnp.int32, (order, order), 1)
    for amount in (4, 2, 1):
        parity = parity ^ (parity >> amount)
    return (1 - 2 * (parity & 1)).astype(jnp.float32).astype(jnp.bfloat16)


def local_kernel(design_ref, signs_ref, out_ref, held, sems):
    def fetch(b):
        rows = pl.ds(b * 128, 128)
        return pltpu.make_async_copy(design_ref.at[rows, :], held.at[rows, :], sems.at[b])

    for b in range(8):
        fetch(b).start()
    table = sylvester(128)
    parts = [[], []]
    for b in range(8):
        fetch(b).wait()
        sign = signs_ref[b : b + 1, :].astype(jnp.float32)
        for half in range(2):
            piece = held[b * 128 : (b + 1) * 128, half * 128 : (half + 1) * 128].T * sign
            high, middle, low = thirds(piece)
            total = jnp.dot(low, table, preferred_element_type=jnp.float32)
            total += jnp.dot(middle, table, preferred_element_type=jnp.float32)
            total += jnp.dot(high, table, preferred_element_type=jnp.float32)
            parts[half].append(total)
    for half in range(2):
        for q, mixed in enumerate(butterflies(parts[half])):
            out_ref[pl.ds(half * 8 + q, 128, stride=16), :] = mixed


def select_kernel(scale, columns_ref, kept_ref, kept_scalar_ref, out_ref, work, first, second):
    for low in range(16):
        mixed = butterflies(columns_ref[high * 16 + low] for high in range(8))
        for high in range(8):
            work[high * 16 + low] = mixed[high]
    for high in range(8):
        mixed = butterflies(work[high * 16 + low] for low in range(16))
        for low in range(16):
            work[high * 16 + low] = mixed[low]
    sublane = lax.broadcasted_iota(jnp.int32, (8, 128), 0)

    def picked(block, lane, key, so_far):
        found = key == sublane + block * 8
        return tuple(
            jnp.where(found, jnp.take_along_axis(work[block, h * 8 : h * 8 + 8, :], lane, axis=1), so_far[h])
            for h in range(2)
        )

    def ids(chunk):
        wanted = jnp.broadcast_to(kept_ref[pl.ds(chunk, 1), :], (8, 128))
        return wanted & 127, wanted >> 7

    zero = jnp.zeros((8, 128), jnp.float32)

    def group(step, carry):
        for inner in range(8):
            chunk = step * 8 + inner
            start = kept_scalar_ref[chunk * 128] >> 10
            lane, key = ids(chunk)
            so_far = (zero, zero)
            for w in range(WINDOW):
                so_far = picked(jnp.minimum(start + w, 127), lane, key, so_far)
            first[pl.ds(chunk, 1), :] = jnp.sum(so_far[0], axis=0, keepdims=True)
            second[pl.ds(chunk, 1), :] = jnp.sum(so_far[1], axis=0, keepdims=True)
        return carry

    lax.fori_loop(0, 8, group, 0)

    def rest(chunk, carry):
        start = (kept_scalar_ref[chunk * 128] >> 10) + WINDOW
        stop = (kept_scalar_ref[chunk * 128 + 127] >> 10) + 1

        @pl.when(stop > start)
        def _():
            lane, key = ids(chunk)
            more = lax.fori_loop(start, stop, lambda block, c: picked(block, lane, key, c), (zero, zero))
            first[pl.ds(chunk, 1), :] += jnp.sum(more[0], axis=0, keepdims=True)
            second[pl.ds(chunk, 1), :] += jnp.sum(more[1], axis=0, keepdims=True)

        return carry

    lax.fori_loop(0, 64, rest, 0)
    left = lax.broadcasted_iota(jnp.int32, (64, 128), 1) < 64
    a, b = first[...] * scale, second[...] * scale
    out_ref[pl.ds(0, 64, stride=2), :] = jnp.where(left, a, pltpu.roll(b, 64, 1))
    out_ref[pl.ds(1, 64, stride=2), :] = jnp.where(left, pltpu.roll(a, 64, 1), b)


def gram_kernel(scale, column_ref, mine_ref, theirs_ref, sketch_ref, out_ref):
    turned, theirs = mine_ref[...].T, theirs_ref[...].T
    own = [turned[:64], turned[64:]]
    other = [theirs[:64], theirs[64:]]
    sketch_ref[:, :128] = own[0]
    sketch_ref[:, 128:] = own[1]
    zero = column_ref[0] == 0

    def choose(a, b):
        return jnp.where(zero, a, b)

    left = choose(own[0], other[1])
    pairs = [
        (own[0], own[0]),
        (own[0], own[1]),
        (own[1], own[1]),
        (left, choose(other[0], own[0])),
        (left, choose(other[1], own[1])),
    ]
    for index, (a, b) in enumerate(pairs):
        out_ref[index * 128 : (index + 1) * 128, :] = scale * lax.dot_general(
            a, b, (((0,), (0,)), ((), ())), precision=lax.Precision.HIGHEST, preferred_element_type=jnp.float32
        )


def copies(shard, axes, count):
    return lax.all_to_all(jnp.broadcast_to(shard[None], (count, *shard.shape)), axes, 0, 0, tiled=True)


def swap_cores(value):
    return lax.ppermute(value, "cols", [(0, 1), (1, 0)])


def thirds(value):
    high = value.astype(jnp.bfloat16)
    rest = value - high.astype(jnp.float32)
    middle = rest.astype(jnp.bfloat16)
    return high, middle, (rest - middle.astype(jnp.float32)).astype(jnp.bfloat16)


def product(left, right):
    (ah, am, al), (bh, bm, bl) = left, right
    top = jnp.concatenate([bh, bm], 0)

    def dot(a, b):
        return lax.dot_general(a, b, (((1,), (0,)), ((), ())), preferred_element_type=jnp.float32)

    small = dot(jnp.concatenate([ah, al], 1), jnp.concatenate([bl, bh], 0))
    small = small + dot(jnp.concatenate([am, am], 1), top)
    return small + dot(jnp.concatenate([ah, ah], 1), top)


def spread(row):
    return jnp.broadcast_to(row, (8, 128))


def block_product(left, right):
    ah, am, al = thirds(left)
    bh, bm, bl = thirds(right)
    return lax.dot_general(
        jnp.concatenate([ah, am, ah, am, al, ah], 0),
        jnp.concatenate([bh, bh, bm, bm, bh, bl], 0),
        (((0,), (0,)), ((), ())),
        preferred_element_type=jnp.float32,
    )


def factor_block(block, upper_ref, inverse_ref, rows_ref, entries_ref, later):
    lanes = lax.broadcasted_iota(jnp.int32, (8, 128), 1)
    strips = [block[8 * s : 8 * s + 8] for s in range(16)]
    for s in range(16):
        here = strips[s]
        base = 8 * s
        rows, entries = rows_ref.at[s % 2], entries_ref.at[s % 2]
        inside = (lanes >= base) & (lanes < base + 8)
        rows[...] = here
        for k in range(8):
            entries[8 * k : 8 * k + 8] = spread(here[:, base + k : base + k + 1])
        e = [[entries[pl.ds(8 * k + i, 8, stride=0), :] if k >= i else None for k in range(8)] for i in range(8)]
        m = [jnp.where(inside, jnp.where(lanes == base + k, 1.0, 0.0), rows[pl.ds(k, 8, stride=0), :]) for k in range(8)]
        d, u, r = [None] * 8, [[None] * 8 for _ in range(8)], [None] * 8
        for k in range(8):
            d[k] = lax.rsqrt(e[k][k])
            for j in range(k + 1, 8):
                u[k][j] = e[k][j] * d[k]
            r[k] = m[k] * d[k]
            for i in range(k + 1, 8):
                for j in range(i, 8):
                    e[i][j] = e[i][j] - u[k][i] * u[k][j]
            for i in range(k + 1, 8):
                m[i] = m[i] - u[k][i] * r[k]
        z = [None] * 8
        for k in reversed(range(8)):
            z[k] = r[k] * d[k]
            for j in reversed(range(k + 1, 8)):
                z[k] = z[k] - (u[k][j] * d[k]) * z[j]
        end = (s // GROUP + 1) * GROUP
        for t in range(s + 1, min(end + AHEAD, 16)):
            there = strips[t]
            total = jnp.where(inside, 0.0, there)
            for k in range(8):
                total = total - spread(there[:, base + k : base + k + 1]) * z[k]
            strips[t] = total
        for k in range(8):
            row = r[k]
            inverse_ref[base + k : base + k + 1, :] = jnp.where(lanes < base + 8, row, 0.0)[:1]
            row = jnp.where(lanes < base + 8, 0.0, row)
            row = jnp.where(lanes == base + k, e[k][k] * d[k], row)
            for j in range(k + 1, 8):
                row = jnp.where(lanes == base + j, u[k][j], row)
            upper_ref[base + k : base + k + 1, :] = row[:1]
        if later:
            later.pop(0)()
        if s + 1 == end and end + AHEAD < 16:
            first, last = 8 * (end - GROUP), 8 * end
            group = lanes[:1] < last
            u_rows = upper_ref[first:last, :]
            delta = block_product(u_rows, jnp.where(group, inverse_ref[first:last, :], u_rows))
            group = (lanes >= first) & (lanes < last)
            for t in range(end + AHEAD, 16):
                strips[t] = jnp.where(group, 0.0, strips[t]) - delta[8 * t : 8 * t + 8]


def cholesky_kernel(column_ref, mine_ref, theirs_ref, out_ref, gram, upper, inverse, rows_ref, entries_ref):
    zero = column_ref[0] == 0
    names = [(0, 0), (0, 1), (1, 1), (0, 2), (0, 3), (2, 2), (2, 3), (3, 3), (1, 2), (1, 3)]
    place = {name: i for i, name in enumerate(names)}
    for i in range(5):
        x, y = mine_ref[i * 128 : i * 128 + 128, :], theirs_ref[i * 128 : i * 128 + 128, :]
        gram[i] = jnp.where(zero, x, y)
        gram[5 + i] = jnp.where(zero, y, x)

    def solve(p, q):
        upper[p * 4 + q] = product(thirds(inverse[p]), thirds(gram[place[p, q]]))

    def update(p, i, j):
        gram[place[i, j]] -= product(thirds(upper[p * 4 + i].T), thirds(upper[p * 4 + j]))

    later = []
    for p in range(4):
        factor_block(gram[place[p, p]], upper.at[p * 4 + p], inverse.at[p], rows_ref, entries_ref, later)
        for work in later:
            work()
        later = []
        for q in range(p):
            upper[p * 4 + q] = jnp.zeros((128, 128), jnp.float32)
        if p < 3:
            solve(p, p + 1)
            update(p, p + 1, p + 1)
        for j in range(p + 2, 4):
            later.append(functools.partial(solve, p, j))
            for i in range(p + 1, j + 1):
                later.append(functools.partial(update, p, i, j))
    for p in range(4):
        for h in range(2):
            out_ref[p * 128 : p * 128 + 128, h * 128 : h * 128 + 128] = jnp.where(zero, upper[p * 4 + h], upper[p * 4 + 2 + h])


def body(design, signs, kept):
    f32 = jnp.float32
    column = lax.axis_index("cols")
    local = pl.pallas_call(
        local_kernel,
        out_shape=jax.ShapeDtypeStruct((2048, 128), f32),
        in_specs=[pl.BlockSpec(memory_space=pltpu.HBM), VMEM],
        out_specs=VMEM,
        scratch_shapes=[pltpu.VMEM((1024, 256), f32), pltpu.SemaphoreType.DMA((8,))],
        compiler_params=pltpu.CompilerParams(vmem_limit_bytes=60 * 1024 * 1024),
        name="local_transform",
    )(design, signs.reshape(8, 128))
    columns = lax.all_to_all(local.reshape(128, 16, 128), ROWS, 0, 0, tiled=True)
    entries = pl.pallas_call(
        functools.partial(select_kernel, 1.0 / math.sqrt(131072)),
        out_shape=jax.ShapeDtypeStruct((128, 128), f32),
        in_specs=[VMEM, VMEM, SMEM],
        out_specs=VMEM,
        scratch_shapes=[
            pltpu.VMEM((128, 16, 128), f32),
            pltpu.VMEM((64, 128), f32),
            pltpu.VMEM((64, 128), f32),
        ],
        compiler_params=LIMIT,
        name="select",
    )(columns, kept.reshape(64, 128), kept)
    entries = lax.all_to_all(entries.reshape(128, 1, 128), ROWS, 0, 0, tiled=True)
    entries = entries.reshape(128, 128)
    sketch, partial = pl.pallas_call(
        functools.partial(gram_kernel, 1.0 / 8192),
        out_shape=(jax.ShapeDtypeStruct((64, 256), f32), jax.ShapeDtypeStruct((640, 128), f32)),
        in_specs=[SMEM, VMEM, VMEM],
        out_specs=(VMEM, VMEM),
        compiler_params=LIMIT,
        name="gram",
    )(column.reshape(1), entries, swap_cores(entries))
    share = jnp.sum(lax.all_to_all(partial.reshape(16, 40, 128), PLANE, 0, 0, tiled=True), axis=0)
    share = jnp.sum(copies(share, "rows_0", 8), axis=0)
    mine = copies(share, PLANE, 16).reshape(640, 128)
    theirs = swap_cores(mine)
    factor = pl.pallas_call(
        cholesky_kernel,
        out_shape=jax.ShapeDtypeStruct((512, 256), f32),
        in_specs=[SMEM, VMEM, VMEM],
        out_specs=VMEM,
        scratch_shapes=[
            pltpu.VMEM((10, 128, 128), f32),
            pltpu.VMEM((16, 128, 128), f32),
            pltpu.VMEM((4, 128, 128), f32),
            pltpu.VMEM((2, 8, 128), f32),
            pltpu.VMEM((2, 64, 128), f32),
        ],
        compiler_params=LIMIT,
        name="cholesky",
    )(column.reshape(1), mine, theirs)
    return sketch, factor


def solution(mesh):
    torus = Mesh(
        mesh.devices.reshape(8, 4, 4, mesh.shape["cols"]), ("rows_0", "rows_1", "rows_2", "cols")
    )
    return jax.shard_map(
        body,
        mesh=torus,
        in_specs=(P(ROWS, "cols"), P(ROWS), P()),
        out_specs=(P(ROWS, "cols"), P(None, "cols")),
        check_vma=False,
    )
```

```python
import functools
import math

import jax
import jax.numpy as jnp
from jax import lax
from jax.experimental import pallas as pl
from jax.experimental.pallas import tpu as pltpu
from jax.sharding import Mesh
from jax.sharding import PartitionSpec as P

ROWS = ("rows_0", "rows_1", "rows_2")
PLANE = ("rows_1", "rows_2")
VMEM = pl.BlockSpec(memory_space=pltpu.VMEM)
SMEM = pl.BlockSpec(memory_space=pltpu.SMEM)
LIMIT = pltpu.CompilerParams(vmem_limit_bytes=32 * 1024 * 1024)
WINDOW = 4
GROUP = 1
AHEAD = 2


def butterflies(values):
    values = list(values)
    half = 1
    while half < len(values):
        for low in range(len(values)):
            if not low & half:
                a, b = values[low], values[low | half]
                values[low], values[low | half] = a + b, a - b
        half *= 2
    return values


def sylvester(order):
    parity = lax.broadcasted_iota(jnp.int32, (order, order), 0)
    parity = parity & lax.broadcasted_iota(jnp.int32, (order, order), 1)
    for amount in (4, 2, 1):
        parity = parity ^ (parity >> amount)
    return (1 - 2 * (parity & 1)).astype(jnp.float32).astype(jnp.bfloat16)


def local_kernel(design_ref, signs_ref, out_ref, held, sems):
    def fetch(b):
        rows = pl.ds(b * 128, 128)
        return pltpu.make_async_copy(design_ref.at[rows, :], held.at[rows, :], sems.at[b])

    for b in range(8):
        fetch(b).start()
    table = sylvester(128)
    parts = [[], []]
    for b in range(8):
        fetch(b).wait()
        sign = signs_ref[b : b + 1, :].astype(jnp.float32)
        for half in range(2):
            piece = held[b * 128 : (b + 1) * 128, half * 128 : (half + 1) * 128].T * sign
            high, middle, low = thirds(piece)
            total = jnp.dot(low, table, preferred_element_type=jnp.float32)
            total += jnp.dot(middle, table, preferred_element_type=jnp.float32)
            total += jnp.dot(high, table, preferred_element_type=jnp.float32)
            parts[half].append(total)
    for half in range(2):
        for q, mixed in enumerate(butterflies(parts[half])):
            out_ref[pl.ds(half * 8 + q, 128, stride=16), :] = mixed


def select_kernel(scale, columns_ref, kept_ref, kept_scalar_ref, out_ref, work, first, second):
    for low in range(16):
        mixed = butterflies(columns_ref[high * 16 + low] for high in range(8))
        for high in range(8):
            work[high * 16 + low] = mixed[high]
    for high in range(8):
        mixed = butterflies(work[high * 16 + low] for low in range(16))
        for low in range(16):
            work[high * 16 + low] = mixed[low]
    sublane = lax.broadcasted_iota(jnp.int32, (8, 128), 0)

    def picked(block, lane, key, so_far):
        found = key == sublane + block * 8
        return tuple(
            jnp.where(found, jnp.take_along_axis(work[block, h * 8 : h * 8 + 8, :], lane, axis=1), so_far[h])
            for h in range(2)
        )

    def ids(chunk):
        wanted = jnp.broadcast_to(kept_ref[pl.ds(chunk, 1), :], (8, 128))
        return wanted & 127, wanted >> 7

    zero = jnp.zeros((8, 128), jnp.float32)

    def group(step, carry):
        for inner in range(8):
            chunk = step * 8 + inner
            start = kept_scalar_ref[chunk * 128] >> 10
            lane, key = ids(chunk)
            so_far = (zero, zero)
            for w in range(WINDOW):
                so_far = picked(jnp.minimum(start + w, 127), lane, key, so_far)
            first[pl.ds(chunk, 1), :] = jnp.sum(so_far[0], axis=0, keepdims=True)
            second[pl.ds(chunk, 1), :] = jnp.sum(so_far[1], axis=0, keepdims=True)
        return carry

    lax.fori_loop(0, 8, group, 0)

    def rest(chunk, carry):
        start = (kept_scalar_ref[chunk * 128] >> 10) + WINDOW
        stop = (kept_scalar_ref[chunk * 128 + 127] >> 10) + 1

        @pl.when(stop > start)
        def _():
            lane, key = ids(chunk)
            more = lax.fori_loop(start, stop, lambda block, c: picked(block, lane, key, c), (zero, zero))
            first[pl.ds(chunk, 1), :] += jnp.sum(more[0], axis=0, keepdims=True)
            second[pl.ds(chunk, 1), :] += jnp.sum(more[1], axis=0, keepdims=True)

        return carry

    lax.fori_loop(0, 64, rest, 0)
    left = lax.broadcasted_iota(jnp.int32, (8, 128), 1) < 64
    for h, chosen in enumerate((first, second)):
        for i in range(4):
            x = chosen[16 * i : 16 * i + 8] * scale
            y = chosen[16 * i + 8 : 16 * i + 16] * scale
            even = jnp.where(left, x, pltpu.roll(y, 64, 1))
            odd = jnp.where(left, pltpu.roll(x, 64, 1), y)
            for z in range(8):
                out_ref[pl.ds(z * 128 + h * 4 + i, 8, stride=16), :] = even
                out_ref[pl.ds(z * 128 + 8 + h * 4 + i, 8, stride=16), :] = odd


def gram_product(a, b):
    ah, am, al = thirds(a)
    bh, bm, bl = thirds(b)
    top = jnp.concatenate([bh, bm], 1)

    def dot(x, y):
        return lax.dot_general(x, y, (((1,), (1,)), ((), ())), preferred_element_type=jnp.float32)

    small = dot(jnp.concatenate([ah, al], 1), jnp.concatenate([bl, bh], 1))
    small = small + dot(jnp.concatenate([am, am], 1), top)
    return small + dot(jnp.concatenate([ah, ah], 1), top)


def gram_kernel(scale, column_ref, z_ref, mine_ref, theirs_ref, sketch_ref, out_ref, turned):
    zero, z = column_ref[0] == 0, z_ref[0]
    for h in range(2):
        turned[...] = mine_ref[pl.ds(h * 4 + z // 2, 128, stride=8), :].T
        sketch_ref[:, h * 128 : h * 128 + 128] = turned[pl.ds(pl.multiple_of(z % 2 * 64, 64), 64), :]

    def wide(ref, h):
        return jnp.concatenate([ref[pl.ds(h * 4 + i, 128, stride=8), :] for i in range(4)], 1)

    def choose(a, b):
        return jnp.where(zero, a, b)

    own = [wide(mine_ref, 0), wide(mine_ref, 1)]
    other = [wide(theirs_ref, 0), wide(theirs_ref, 1)]
    both = jnp.concatenate(own, 0)
    square = gram_product(both, both) * scale
    right = jnp.concatenate([choose(other[0], own[0]), choose(other[1], own[1])], 0)
    cross = gram_product(choose(own[0], other[1]), right) * scale
    blocks = [square[:128, :128], square[:128, 128:], square[128:, 128:], cross[:, :128], cross[:, 128:]]
    for index, block in enumerate(blocks):
        out_ref[index * 128 : (index + 1) * 128, :] = block


def copies(shard, axes, count):
    return lax.all_to_all(jnp.broadcast_to(shard[None], (count, *shard.shape)), axes, 0, 0, tiled=True)


def swap_cores(value):
    return lax.ppermute(value, "cols", [(0, 1), (1, 0)])


def thirds(value):
    high = value.astype(jnp.bfloat16)
    rest = value - high.astype(jnp.float32)
    middle = rest.astype(jnp.bfloat16)
    return high, middle, (rest - middle.astype(jnp.float32)).astype(jnp.bfloat16)


def product(left, right):
    (ah, am, al), (bh, bm, bl) = left, right
    top = jnp.concatenate([bh, bm], 0)

    def dot(a, b):
        return lax.dot_general(a, b, (((1,), (0,)), ((), ())), preferred_element_type=jnp.float32)

    small = dot(jnp.concatenate([ah, al], 1), jnp.concatenate([bl, bh], 0))
    small = small + dot(jnp.concatenate([am, am], 1), top)
    return small + dot(jnp.concatenate([ah, ah], 1), top)


def spread(row):
    return jnp.broadcast_to(row, (8, 128))


def block_product(left, right):
    ah, am, al = thirds(left)
    bh, bm, bl = thirds(right)
    return lax.dot_general(
        jnp.concatenate([ah, am, ah, am, al, ah], 0),
        jnp.concatenate([bh, bh, bm, bm, bh, bl], 0),
        (((0,), (0,)), ((), ())),
        preferred_element_type=jnp.float32,
    )


def factor_block(block, upper_ref, inverse_ref, rows_ref, entries_ref, later):
    lanes = lax.broadcasted_iota(jnp.int32, (8, 128), 1)
    strips = [block[8 * s : 8 * s + 8] for s in range(16)]
    for s in range(16):
        here = strips[s]
        base = 8 * s
        rows, entries = rows_ref.at[s % 2], entries_ref.at[s % 2]
        inside = (lanes >= base) & (lanes < base + 8)
        rows[...] = here
        for k in range(8):
            entries[8 * k : 8 * k + 8] = spread(here[:, base + k : base + k + 1])
        e = [[entries[pl.ds(8 * k + i, 8, stride=0), :] if k >= i else None for k in range(8)] for i in range(8)]
        m = [jnp.where(inside, jnp.where(lanes == base + k, 1.0, 0.0), rows[pl.ds(k, 8, stride=0), :]) for k in range(8)]
        d, u, r = [None] * 8, [[None] * 8 for _ in range(8)], [None] * 8
        for k in range(8):
            d[k] = lax.rsqrt(e[k][k])
            for j in range(k + 1, 8):
                u[k][j] = e[k][j] * d[k]
            r[k] = m[k] * d[k]
            for i in range(k + 1, 8):
                for j in range(i, 8):
                    e[i][j] = e[i][j] - u[k][i] * u[k][j]
            for i in range(k + 1, 8):
                m[i] = m[i] - u[k][i] * r[k]
        z = [None] * 8
        for k in reversed(range(8)):
            z[k] = r[k] * d[k]
            for j in reversed(range(k + 1, 8)):
                z[k] = z[k] - (u[k][j] * d[k]) * z[j]
        end = (s // GROUP + 1) * GROUP
        for t in range(s + 1, min(end + AHEAD, 16)):
            there = strips[t]
            total = jnp.where(inside, 0.0, there)
            for k in range(8):
                total = total - spread(there[:, base + k : base + k + 1]) * z[k]
            strips[t] = total
        for k in range(8):
            row = r[k]
            inverse_ref[base + k : base + k + 1, :] = jnp.where(lanes < base + 8, row, 0.0)[:1]
            row = jnp.where(lanes < base + 8, 0.0, row)
            row = jnp.where(lanes == base + k, e[k][k] * d[k], row)
            for j in range(k + 1, 8):
                row = jnp.where(lanes == base + j, u[k][j], row)
            upper_ref[base + k : base + k + 1, :] = row[:1]
        if later:
            later.pop(0)()
        if s + 1 == end and end + AHEAD < 16:
            first, last = 8 * (end - GROUP), 8 * end
            group = lanes[:1] < last
            u_rows = upper_ref[first:last, :]
            delta = block_product(u_rows, jnp.where(group, inverse_ref[first:last, :], u_rows))
            group = (lanes >= first) & (lanes < last)
            for t in range(end + AHEAD, 16):
                strips[t] = jnp.where(group, 0.0, strips[t]) - delta[8 * t : 8 * t + 8]


def cholesky_kernel(column_ref, mine_ref, theirs_ref, out_ref, gram, upper, inverse, rows_ref, entries_ref):
    zero = column_ref[0] == 0
    names = [(0, 0), (0, 1), (1, 1), (0, 2), (0, 3), (2, 2), (2, 3), (3, 3), (1, 2), (1, 3)]
    place = {name: i for i, name in enumerate(names)}
    for i in range(5):
        x, y = mine_ref[i * 128 : i * 128 + 128, :], theirs_ref[i * 128 : i * 128 + 128, :]
        gram[i] = jnp.where(zero, x, y)
        gram[5 + i] = jnp.where(zero, y, x)

    def solve(p, q):
        upper[p * 4 + q] = product(thirds(inverse[p]), thirds(gram[place[p, q]]))

    def update(p, i, j):
        gram[place[i, j]] -= product(thirds(upper[p * 4 + i].T), thirds(upper[p * 4 + j]))

    later = []
    for p in range(4):
        factor_block(gram[place[p, p]], upper.at[p * 4 + p], inverse.at[p], rows_ref, entries_ref, later)
        for work in later:
            work()
        later = []
        for q in range(p):
            upper[p * 4 + q] = jnp.zeros((128, 128), jnp.float32)
        if p < 3:
            solve(p, p + 1)
            update(p, p + 1, p + 1)
        for j in range(p + 2, 4):
            later.append(functools.partial(solve, p, j))
            for i in range(p + 1, j + 1):
                later.append(functools.partial(update, p, i, j))
    for p in range(4):
        for h in range(2):
            out_ref[p * 128 : p * 128 + 128, h * 128 : h * 128 + 128] = jnp.where(zero, upper[p * 4 + h], upper[p * 4 + 2 + h])


def body(design, signs, kept):
    f32 = jnp.float32
    column = lax.axis_index("cols")
    local = pl.pallas_call(
        local_kernel,
        out_shape=jax.ShapeDtypeStruct((2048, 128), f32),
        in_specs=[pl.BlockSpec(memory_space=pltpu.HBM), VMEM],
        out_specs=VMEM,
        scratch_shapes=[pltpu.VMEM((1024, 256), f32), pltpu.SemaphoreType.DMA((8,))],
        compiler_params=pltpu.CompilerParams(vmem_limit_bytes=52 * 1024 * 1024 + 256 * 1024),
        name="local_transform",
    )(design, signs.reshape(8, 128))
    columns = lax.all_to_all(local.reshape(128, 16, 128), ROWS, 0, 0, tiled=True)
    entries = pl.pallas_call(
        functools.partial(select_kernel, 1.0 / math.sqrt(131072)),
        out_shape=jax.ShapeDtypeStruct((1024, 128), f32),
        in_specs=[VMEM, VMEM, SMEM],
        out_specs=VMEM,
        scratch_shapes=[
            pltpu.VMEM((128, 16, 128), f32),
            pltpu.VMEM((64, 128), f32),
            pltpu.VMEM((64, 128), f32),
        ],
        compiler_params=LIMIT,
        name="select",
    )(columns, kept.reshape(64, 128), kept)
    entries = lax.all_to_all(entries.reshape(128, 8, 128), ROWS, 0, 0, tiled=True).reshape(1024, 128)
    sketch, partial = pl.pallas_call(
        functools.partial(gram_kernel, 1.0 / 8192),
        out_shape=(jax.ShapeDtypeStruct((64, 256), f32), jax.ShapeDtypeStruct((640, 128), f32)),
        in_specs=[SMEM, SMEM, VMEM, VMEM],
        out_specs=(VMEM, VMEM),
        scratch_shapes=[pltpu.VMEM((128, 128), f32)],
        compiler_params=LIMIT,
        name="gram",
    )(column.reshape(1), lax.axis_index("rows_0").reshape(1), entries, swap_cores(entries))
    share = jnp.sum(lax.all_to_all(partial.reshape(16, 40, 128), PLANE, 0, 0, tiled=True), axis=0)
    mine = copies(share, PLANE, 16).reshape(640, 128)
    theirs = swap_cores(mine)
    factor = pl.pallas_call(
        cholesky_kernel,
        out_shape=jax.ShapeDtypeStruct((512, 256), f32),
        in_specs=[SMEM, VMEM, VMEM],
        out_specs=VMEM,
        scratch_shapes=[
            pltpu.VMEM((10, 128, 128), f32),
            pltpu.VMEM((16, 128, 128), f32),
            pltpu.VMEM((4, 128, 128), f32),
            pltpu.VMEM((2, 8, 128), f32),
            pltpu.VMEM((2, 64, 128), f32),
        ],
        compiler_params=LIMIT,
        name="cholesky",
    )(column.reshape(1), mine, theirs)
    return sketch, factor


def solution(mesh):
    torus = Mesh(
        mesh.devices.reshape(8, 4, 4, mesh.shape["cols"]), ("rows_0", "rows_1", "rows_2", "cols")
    )
    return jax.shard_map(
        body,
        mesh=torus,
        in_specs=(P(ROWS, "cols"), P(ROWS), P()),
        out_specs=(P(ROWS, "cols"), P(None, "cols")),
        check_vma=False,
    )
```

```python
import functools
import math

import jax
import jax.numpy as jnp
from jax import lax
from jax.experimental import pallas as pl
from jax.experimental.pallas import tpu as pltpu
from jax.sharding import Mesh
from jax.sharding import PartitionSpec as P

ROWS = ("rows_0", "rows_1", "rows_2")
PLANE = ("rows_1", "rows_2")
VMEM = pl.BlockSpec(memory_space=pltpu.VMEM)
SMEM = pl.BlockSpec(memory_space=pltpu.SMEM)
LIMIT = pltpu.CompilerParams(vmem_limit_bytes=32 * 1024 * 1024)
WINDOW = 4
GROUP = 1
AHEAD = 2


def butterflies(values):
    values = list(values)
    half = 1
    while half < len(values):
        for low in range(len(values)):
            if not low & half:
                a, b = values[low], values[low | half]
                values[low], values[low | half] = a + b, a - b
        half *= 2
    return values


def sylvester(order):
    parity = lax.broadcasted_iota(jnp.int32, (order, order), 0)
    parity = parity & lax.broadcasted_iota(jnp.int32, (order, order), 1)
    for amount in (4, 2, 1):
        parity = parity ^ (parity >> amount)
    return (1 - 2 * (parity & 1)).astype(jnp.float32).astype(jnp.bfloat16)


def local_kernel(design_ref, signs_ref, out_ref):
    table = sylvester(128)
    for half in range(2):
        parts = []
        for b in range(8):
            piece = design_ref[b * 128 : (b + 1) * 128, half * 128 : (half + 1) * 128].T
            high, middle, low = thirds(piece * signs_ref[b : b + 1, :])
            total = jnp.dot(low, table, preferred_element_type=jnp.float32)
            total += jnp.dot(middle, table, preferred_element_type=jnp.float32)
            total += jnp.dot(high, table, preferred_element_type=jnp.float32)
            parts.append(total)
        for q, mixed in enumerate(butterflies(parts)):
            out_ref[pl.ds(half * 8 + q, 128, stride=16), :] = mixed


def select_kernel(scale, columns_ref, kept_ref, kept_scalar_ref, out_ref, work, first, second):
    for low in range(16):
        mixed = butterflies(columns_ref[high * 16 + low] for high in range(8))
        for high in range(8):
            work[high * 16 + low] = mixed[high]
    for high in range(8):
        mixed = butterflies(work[high * 16 + low] for low in range(16))
        for low in range(16):
            work[high * 16 + low] = mixed[low]
    sublane = lax.broadcasted_iota(jnp.int32, (8, 128), 0)

    def picked(block, lane, key, so_far):
        found = key == sublane + block * 8
        return tuple(
            jnp.where(found, jnp.take_along_axis(work[block, h * 8 : h * 8 + 8, :], lane, axis=1), so_far[h])
            for h in range(2)
        )

    def ids(chunk):
        wanted = jnp.broadcast_to(kept_ref[pl.ds(chunk, 1), :], (8, 128))
        return wanted & 127, wanted >> 7

    zero = jnp.zeros((8, 128), jnp.float32)

    def merged(values):
        for bit in (1, 2, 4):
            low = (sublane & bit) == 0
            values = [
                jnp.where(low, x, y) + pltpu.roll(jnp.where(low, y, x), 8 - bit, 0)
                for x, y in zip(values[::2], values[1::2])
            ]
        return values[0]

    def group(step, carry):
        sums = [[], []]
        for inner in range(8):
            chunk = step * 8 + inner
            start = kept_scalar_ref[chunk * 128] >> 10
            lane, key = ids(chunk)
            so_far = (zero, zero)
            for w in range(WINDOW):
                so_far = picked(jnp.minimum(start + w, 127), lane, key, so_far)
            sums[0].append(so_far[0])
            sums[1].append(so_far[1])
        rows = pl.ds(pl.multiple_of(step * 8, 8), 8)
        first[rows, :] = merged(sums[0])
        second[rows, :] = merged(sums[1])
        return carry

    lax.fori_loop(0, 8, group, 0)

    def rest(chunk, carry):
        start = (kept_scalar_ref[chunk * 128] >> 10) + WINDOW
        stop = (kept_scalar_ref[chunk * 128 + 127] >> 10) + 1

        @pl.when(stop > start)
        def _():
            lane, key = ids(chunk)
            more = lax.fori_loop(start, stop, lambda block, c: picked(block, lane, key, c), (zero, zero))
            first[pl.ds(chunk, 1), :] += jnp.sum(more[0], axis=0, keepdims=True)
            second[pl.ds(chunk, 1), :] += jnp.sum(more[1], axis=0, keepdims=True)

        return carry

    lax.fori_loop(0, 64, rest, 0)
    left = lax.broadcasted_iota(jnp.int32, (8, 128), 1) < 64
    for h, chosen in enumerate((first, second)):
        for i in range(4):
            x = chosen[16 * i : 16 * i + 8] * scale
            y = chosen[16 * i + 8 : 16 * i + 16] * scale
            even = jnp.where(left, x, pltpu.roll(y, 64, 1))
            odd = jnp.where(left, pltpu.roll(x, 64, 1), y)
            for z in range(8):
                out_ref[pl.ds(z * 128 + h * 4 + i, 8, stride=16), :] = even
                out_ref[pl.ds(z * 128 + 8 + h * 4 + i, 8, stride=16), :] = odd


def gram_product(a, b):
    ah, am, al = thirds(a)
    bh, bm, bl = thirds(b)
    top = jnp.concatenate([bh, bm], 1)

    def dot(x, y):
        return lax.dot_general(x, y, (((1,), (1,)), ((), ())), preferred_element_type=jnp.float32)

    small = dot(jnp.concatenate([ah, al], 1), jnp.concatenate([bl, bh], 1))
    small = small + dot(jnp.concatenate([am, am], 1), top)
    return small + dot(jnp.concatenate([ah, ah], 1), top)


def wide(ref, h):
    return jnp.concatenate([ref[pl.ds(h * 4 + i, 128, stride=8), :] for i in range(4)], 1)


def own_kernel(scale, z_ref, mine_ref, sketch_ref, out_ref, turned):
    z = z_ref[0]
    for h in range(2):
        turned[...] = mine_ref[pl.ds(h * 4 + z // 2, 128, stride=8), :].T
        sketch_ref[:, h * 128 : h * 128 + 128] = turned[pl.ds(pl.multiple_of(z % 2 * 64, 64), 64), :]
    both = jnp.concatenate([wide(mine_ref, 0), wide(mine_ref, 1)], 0)
    square = gram_product(both, both) * scale
    for index, block in enumerate([square[:128, :128], square[:128, 128:], square[128:, 128:]]):
        out_ref[index * 128 : (index + 1) * 128, :] = block


def cross_kernel(scale, column_ref, mine_ref, theirs_ref, blocks_ref, out_ref):
    zero = column_ref[0] == 0

    def choose(a, b):
        return jnp.where(zero, a, b)

    own = [wide(mine_ref, 0), wide(mine_ref, 1)]
    other = [wide(theirs_ref, 0), wide(theirs_ref, 1)]
    right = jnp.concatenate([choose(other[0], own[0]), choose(other[1], own[1])], 0)
    cross = gram_product(choose(own[0], other[1]), right) * scale
    out_ref[:384, :] = blocks_ref[...]
    out_ref[384:512, :] = cross[:, :128]
    out_ref[512:, :] = cross[:, 128:]


def copies(shard, axes, count):
    return lax.all_to_all(jnp.broadcast_to(shard[None], (count, *shard.shape)), axes, 0, 0, tiled=True)


def swap_cores(value):
    return lax.ppermute(value, "cols", [(0, 1), (1, 0)])


def thirds(value):
    high = value.astype(jnp.bfloat16)
    rest = value - high.astype(jnp.float32)
    middle = rest.astype(jnp.bfloat16)
    return high, middle, (rest - middle.astype(jnp.float32)).astype(jnp.bfloat16)


def product(left, right):
    (ah, am, al), (bh, bm, bl) = left, right
    top = jnp.concatenate([bh, bm], 0)

    def dot(a, b):
        return lax.dot_general(a, b, (((1,), (0,)), ((), ())), preferred_element_type=jnp.float32)

    small = dot(jnp.concatenate([ah, al], 1), jnp.concatenate([bl, bh], 0))
    small = small + dot(jnp.concatenate([am, am], 1), top)
    return small + dot(jnp.concatenate([ah, ah], 1), top)


def spread(row):
    return jnp.broadcast_to(row, (8, 128))


def block_product(left, right):
    ah, am, al = thirds(left)
    bh, bm, bl = thirds(right)
    return lax.dot_general(
        jnp.concatenate([ah, am, ah, am, al, ah], 0),
        jnp.concatenate([bh, bh, bm, bm, bh, bl], 0),
        (((0,), (0,)), ((), ())),
        preferred_element_type=jnp.float32,
    )


def factor_block(block, upper_ref, inverse_ref, rows_ref, entries_ref, later):
    lanes = lax.broadcasted_iota(jnp.int32, (8, 128), 1)
    strips = [block[8 * s : 8 * s + 8] for s in range(16)]
    for s in range(16):
        here = strips[s]
        base = 8 * s
        rows, entries = rows_ref.at[s % 2], entries_ref.at[s % 2]
        inside = (lanes >= base) & (lanes < base + 8)
        rows[...] = here
        for k in range(8):
            entries[8 * k : 8 * k + 8] = spread(here[:, base + k : base + k + 1])
        e = [[entries[pl.ds(8 * k + i, 8, stride=0), :] if k >= i else None for k in range(8)] for i in range(8)]
        m = [jnp.where(inside, jnp.where(lanes == base + k, 1.0, 0.0), rows[pl.ds(k, 8, stride=0), :]) for k in range(8)]
        d, u, r = [None] * 8, [[None] * 8 for _ in range(8)], [None] * 8
        for k in range(8):
            d[k] = lax.rsqrt(e[k][k])
            for j in range(k + 1, 8):
                u[k][j] = e[k][j] * d[k]
            r[k] = m[k] * d[k]
            for i in range(k + 1, 8):
                for j in range(i, 8):
                    e[i][j] = e[i][j] - u[k][i] * u[k][j]
            for i in range(k + 1, 8):
                m[i] = m[i] - u[k][i] * r[k]
        z = [None] * 8
        for k in reversed(range(8)):
            z[k] = r[k] * d[k]
            for j in reversed(range(k + 1, 8)):
                z[k] = z[k] - (u[k][j] * d[k]) * z[j]
        end = (s // GROUP + 1) * GROUP
        for t in range(s + 1, min(end + AHEAD, 16)):
            there = strips[t]
            total = jnp.where(inside, 0.0, there)
            for k in range(8):
                total = total - spread(there[:, base + k : base + k + 1]) * z[k]
            strips[t] = total
        for k in range(8):
            row = r[k]
            inverse_ref[base + k : base + k + 1, :] = jnp.where(lanes < base + 8, row, 0.0)[:1]
            row = jnp.where(lanes < base + 8, 0.0, row)
            row = jnp.where(lanes == base + k, e[k][k] * d[k], row)
            for j in range(k + 1, 8):
                row = jnp.where(lanes == base + j, u[k][j], row)
            upper_ref[base + k : base + k + 1, :] = row[:1]
        if later:
            later.pop(0)()
        if s + 1 == end and end + AHEAD < 16:
            first, last = 8 * (end - GROUP), 8 * end
            group = lanes[:1] < last
            u_rows = upper_ref[first:last, :]
            delta = block_product(u_rows, jnp.where(group, inverse_ref[first:last, :], u_rows))
            group = (lanes >= first) & (lanes < last)
            for t in range(end + AHEAD, 16):
                strips[t] = jnp.where(group, 0.0, strips[t]) - delta[8 * t : 8 * t + 8]


def cholesky_kernel(column_ref, mine_ref, theirs_ref, out_ref, gram, upper, inverse, rows_ref, entries_ref):
    zero = column_ref[0] == 0
    names = [(0, 0), (0, 1), (1, 1), (0, 2), (0, 3), (2, 2), (2, 3), (3, 3), (1, 2), (1, 3)]
    place = {name: i for i, name in enumerate(names)}
    for i in range(5):
        x, y = mine_ref[i * 128 : i * 128 + 128, :], theirs_ref[i * 128 : i * 128 + 128, :]
        gram[i] = jnp.where(zero, x, y)
        gram[5 + i] = jnp.where(zero, y, x)

    def solve(p, q):
        upper[p * 4 + q] = product(thirds(inverse[p]), thirds(gram[place[p, q]]))

    def update(p, i, j):
        gram[place[i, j]] -= product(thirds(upper[p * 4 + i].T), thirds(upper[p * 4 + j]))

    later = []
    for p in range(4):
        factor_block(gram[place[p, p]], upper.at[p * 4 + p], inverse.at[p], rows_ref, entries_ref, later)
        for work in later:
            work()
        later = []
        for q in range(p):
            upper[p * 4 + q] = jnp.zeros((128, 128), jnp.float32)
        if p < 3:
            solve(p, p + 1)
            update(p, p + 1, p + 1)
        for j in range(p + 2, 4):
            later.append(functools.partial(solve, p, j))
            for i in range(p + 1, j + 1):
                later.append(functools.partial(update, p, i, j))
    for p in range(4):
        for h in range(2):
            out_ref[p * 128 : p * 128 + 128, h * 128 : h * 128 + 128] = jnp.where(zero, upper[p * 4 + h], upper[p * 4 + 2 + h])


def body(design, signs, kept):
    f32 = jnp.float32
    column = lax.axis_index("cols")
    local = pl.pallas_call(
        local_kernel,
        out_shape=jax.ShapeDtypeStruct((2048, 128), f32),
        in_specs=[VMEM, VMEM],
        out_specs=VMEM,
        compiler_params=LIMIT,
        name="local_transform",
    )(design, signs.astype(f32).reshape(8, 128))
    columns = lax.all_to_all(local.reshape(128, 16, 128), ROWS, 0, 0, tiled=True)
    entries = pl.pallas_call(
        functools.partial(select_kernel, 1.0 / math.sqrt(131072)),
        out_shape=jax.ShapeDtypeStruct((1024, 128), f32),
        in_specs=[VMEM, VMEM, SMEM],
        out_specs=VMEM,
        scratch_shapes=[
            pltpu.VMEM((128, 16, 128), f32),
            pltpu.VMEM((64, 128), f32),
            pltpu.VMEM((64, 128), f32),
        ],
        compiler_params=LIMIT,
        name="select",
    )(columns, kept.reshape(64, 128), kept)
    entries = lax.all_to_all(entries.reshape(128, 8, 128), ROWS, 0, 0, tiled=True).reshape(1024, 128)
    theirs = swap_cores(entries)
    sketch, blocks = pl.pallas_call(
        functools.partial(own_kernel, 1.0 / 8192),
        out_shape=(jax.ShapeDtypeStruct((64, 256), f32), jax.ShapeDtypeStruct((384, 128), f32)),
        in_specs=[SMEM, VMEM],
        out_specs=(VMEM, VMEM),
        scratch_shapes=[pltpu.VMEM((128, 128), f32)],
        compiler_params=LIMIT,
        cost_estimate=pl.CostEstimate(flops=800_000_000, bytes_accessed=1_000_000, transcendentals=0),
        name="own_gram",
    )(lax.axis_index("rows_0").reshape(1), entries)
    partial = pl.pallas_call(
        functools.partial(cross_kernel, 1.0 / 8192),
        out_shape=jax.ShapeDtypeStruct((640, 128), f32),
        in_specs=[SMEM, VMEM, VMEM, VMEM],
        out_specs=VMEM,
        compiler_params=LIMIT,
        name="cross_gram",
    )(column.reshape(1), entries, theirs, blocks)
    share = jnp.sum(lax.all_to_all(partial.reshape(16, 40, 128), PLANE, 0, 0, tiled=True), axis=0)
    mine = copies(share, PLANE, 16).reshape(640, 128)
    theirs = swap_cores(mine)
    factor = pl.pallas_call(
        cholesky_kernel,
        out_shape=jax.ShapeDtypeStruct((512, 256), f32),
        in_specs=[SMEM, VMEM, VMEM],
        out_specs=VMEM,
        scratch_shapes=[
            pltpu.VMEM((10, 128, 128), f32),
            pltpu.VMEM((16, 128, 128), f32),
            pltpu.VMEM((4, 128, 128), f32),
            pltpu.VMEM((2, 8, 128), f32),
            pltpu.VMEM((2, 64, 128), f32),
        ],
        compiler_params=LIMIT,
        name="cholesky",
    )(column.reshape(1), mine, theirs)
    return sketch, factor


def solution(mesh):
    torus = Mesh(
        mesh.devices.reshape(8, 4, 4, mesh.shape["cols"]), ("rows_0", "rows_1", "rows_2", "cols")
    )
    return jax.shard_map(
        body,
        mesh=torus,
        in_specs=(P(ROWS, "cols"), P(ROWS), P()),
        out_specs=(P(ROWS, "cols"), P(None, "cols")),
        check_vma=False,
    )
```

```python
import functools
import math

import jax
import jax.numpy as jnp
from jax import lax
from jax.experimental import pallas as pl
from jax.experimental.pallas import tpu as pltpu
from jax.sharding import Mesh
from jax.sharding import PartitionSpec as P

ROWS = ("rows_0", "rows_1", "rows_2")
PLANE = ("rows_1", "rows_2")
VMEM = pl.BlockSpec(memory_space=pltpu.VMEM)
SMEM = pl.BlockSpec(memory_space=pltpu.SMEM)
LIMIT = pltpu.CompilerParams(vmem_limit_bytes=32 * 1024 * 1024)
WINDOW = 4
GROUP = 2
AHEAD = 2


def butterflies(values):
    values = list(values)
    half = 1
    while half < len(values):
        for low in range(len(values)):
            if not low & half:
                a, b = values[low], values[low | half]
                values[low], values[low | half] = a + b, a - b
        half *= 2
    return values


def sylvester(order):
    parity = lax.broadcasted_iota(jnp.int32, (order, order), 0)
    parity = parity & lax.broadcasted_iota(jnp.int32, (order, order), 1)
    for amount in (4, 2, 1):
        parity = parity ^ (parity >> amount)
    return (1 - 2 * (parity & 1)).astype(jnp.float32).astype(jnp.bfloat16)


def local_kernel(design_ref, signs_ref, out_ref):
    table = sylvester(128)
    for half in range(2):
        parts = []
        for b in range(8):
            piece = design_ref[b * 128 : (b + 1) * 128, half * 128 : (half + 1) * 128].T
            high, middle, low = thirds(piece * signs_ref[b : b + 1, :])
            total = jnp.dot(low, table, preferred_element_type=jnp.float32)
            total += jnp.dot(middle, table, preferred_element_type=jnp.float32)
            total += jnp.dot(high, table, preferred_element_type=jnp.float32)
            parts.append(total)
        for q, mixed in enumerate(butterflies(parts)):
            out_ref[pl.ds(half * 8 + q, 128, stride=16), :] = mixed


def select_kernel(scale, columns_ref, kept_ref, kept_any_ref, out_ref, work, first, second, kept_scalar_ref, sem):
    fetch = pltpu.make_async_copy(kept_any_ref, kept_scalar_ref, sem)
    fetch.start()
    for low in range(16):
        mixed = butterflies(columns_ref[high * 16 + low] for high in range(8))
        for high in range(8):
            work[high * 16 + low] = mixed[high]
    for high in range(8):
        mixed = butterflies(work[high * 16 + low] for low in range(16))
        for low in range(16):
            work[high * 16 + low] = mixed[low]
    fetch.wait()
    sublane = lax.broadcasted_iota(jnp.int32, (8, 128), 0)

    def picked(block, lane, key, so_far):
        found = key == sublane + block * 8
        return tuple(
            jnp.where(found, jnp.take_along_axis(work[block, h * 8 : h * 8 + 8, :], lane, axis=1), so_far[h])
            for h in range(2)
        )

    def ids(chunk):
        wanted = jnp.broadcast_to(kept_ref[pl.ds(chunk, 1), :], (8, 128))
        return wanted & 127, wanted >> 7

    zero = jnp.zeros((8, 128), jnp.float32)

    def merged(values):
        for bit in (1, 2, 4):
            low = (sublane & bit) == 0
            values = [
                jnp.where(low, x, y) + pltpu.roll(jnp.where(low, y, x), 8 - bit, 0)
                for x, y in zip(values[::2], values[1::2])
            ]
        return values[0]

    def group(step, widest):
        sums = [[], []]
        for inner in range(8):
            chunk = step * 8 + inner
            start = kept_scalar_ref[chunk * 128] >> 10
            widest = jnp.maximum(widest, (kept_scalar_ref[chunk * 128 + 127] >> 10) - start)
            lane, key = ids(chunk)
            so_far = (zero, zero)
            for w in range(WINDOW):
                so_far = picked(jnp.minimum(start + w, 127), lane, key, so_far)
            sums[0].append(so_far[0])
            sums[1].append(so_far[1])
        rows = pl.ds(pl.multiple_of(step * 8, 8), 8)
        first[rows, :] = merged(sums[0])
        second[rows, :] = merged(sums[1])
        return widest

    widest = lax.fori_loop(0, 8, group, 0, unroll=True)

    def rest(chunk, carry):
        start = (kept_scalar_ref[chunk * 128] >> 10) + WINDOW
        stop = (kept_scalar_ref[chunk * 128 + 127] >> 10) + 1

        @pl.when(stop > start)
        def _():
            lane, key = ids(chunk)
            more = lax.fori_loop(start, stop, lambda block, c: picked(block, lane, key, c), (zero, zero))
            first[pl.ds(chunk, 1), :] += jnp.sum(more[0], axis=0, keepdims=True)
            second[pl.ds(chunk, 1), :] += jnp.sum(more[1], axis=0, keepdims=True)

        return carry

    @pl.when(widest >= WINDOW)
    def _():
        lax.fori_loop(0, 64, rest, 0)

    left = lax.broadcasted_iota(jnp.int32, (8, 128), 1) < 64
    for h, chosen in enumerate((first, second)):
        for i in range(4):
            x = chosen[16 * i : 16 * i + 8] * scale
            y = chosen[16 * i + 8 : 16 * i + 16] * scale
            even = jnp.where(left, x, pltpu.roll(y, 64, 1))
            odd = jnp.where(left, pltpu.roll(x, 64, 1), y)
            for z in range(8):
                out_ref[pl.ds(z * 128 + h * 4 + i, 8, stride=16), :] = even
                out_ref[pl.ds(z * 128 + 8 + h * 4 + i, 8, stride=16), :] = odd


def gram_product(a, b):
    ah, am, al = thirds(a)
    bh, bm, bl = thirds(b)
    top = jnp.concatenate([bh, bm], 1)

    def dot(x, y):
        return lax.dot_general(x, y, (((1,), (1,)), ((), ())), preferred_element_type=jnp.float32)

    small = dot(jnp.concatenate([ah, al], 1), jnp.concatenate([bl, bh], 1))
    small = small + dot(jnp.concatenate([am, am], 1), top)
    return small + dot(jnp.concatenate([ah, ah], 1), top)


def wide(ref, h):
    return jnp.concatenate([ref[pl.ds(h * 4 + i, 128, stride=8), :] for i in range(4)], 1)


def own_kernel(scale, z_ref, mine_ref, sketch_ref, out_ref, turned):
    z = z_ref[0]
    for h in range(2):
        turned[...] = mine_ref[pl.ds(h * 4 + z // 2, 128, stride=8), :].T
        sketch_ref[:, h * 128 : h * 128 + 128] = turned[pl.ds(pl.multiple_of(z % 2 * 64, 64), 64), :]
    both = jnp.concatenate([wide(mine_ref, 0), wide(mine_ref, 1)], 0)
    square = gram_product(both, both) * scale
    for index, block in enumerate([square[:128, :128], square[:128, 128:], square[128:, 128:]]):
        out_ref[index * 128 : (index + 1) * 128, :] = block


def cross_kernel(scale, column_ref, mine_ref, theirs_ref, blocks_ref, out_ref):
    zero = column_ref[0] == 0

    def choose(a, b):
        return jnp.where(zero, a, b)

    own = [wide(mine_ref, 0), wide(mine_ref, 1)]
    other = [wide(theirs_ref, 0), wide(theirs_ref, 1)]
    right = jnp.concatenate([choose(other[0], own[0]), choose(other[1], own[1])], 0)
    cross = gram_product(choose(own[0], other[1]), right) * scale
    out_ref[:384, :] = blocks_ref[...]
    out_ref[384:512, :] = cross[:, :128]
    out_ref[512:, :] = cross[:, 128:]


def copies(shard, axes, count):
    return lax.all_to_all(jnp.broadcast_to(shard[None], (count, *shard.shape)), axes, 0, 0, tiled=True)


def swap_cores(value):
    return lax.ppermute(value, "cols", [(0, 1), (1, 0)])


def thirds(value):
    high = value.astype(jnp.bfloat16)
    rest = value - high.astype(jnp.float32)
    middle = rest.astype(jnp.bfloat16)
    return high, middle, (rest - middle.astype(jnp.float32)).astype(jnp.bfloat16)


def product(left, right):
    (ah, am, al), (bh, bm, bl) = left, right
    top = jnp.concatenate([bh, bm], 0)

    def dot(a, b):
        return lax.dot_general(a, b, (((1,), (0,)), ((), ())), preferred_element_type=jnp.float32)

    small = dot(jnp.concatenate([ah, al], 1), jnp.concatenate([bl, bh], 0))
    small = small + dot(jnp.concatenate([am, am], 1), top)
    return small + dot(jnp.concatenate([ah, ah], 1), top)


def spread(row):
    return jnp.broadcast_to(row, (8, 128))


def block_product(left, right):
    ah, am, al = thirds(left)
    bh, bm, bl = thirds(right)
    return lax.dot_general(
        jnp.concatenate([ah, am, ah, am, al, ah], 0),
        jnp.concatenate([bh, bh, bm, bm, bh, bl], 0),
        (((0,), (0,)), ((), ())),
        preferred_element_type=jnp.float32,
    )


def factor_block(block, upper_ref, inverse_ref, rows_ref, entries_ref, later):
    lanes = lax.broadcasted_iota(jnp.int32, (8, 128), 1)
    strips = [block[8 * s : 8 * s + 8] for s in range(16)]
    for s in range(16):
        here = strips[s]
        base = 8 * s
        rows, entries = rows_ref.at[s % 2], entries_ref.at[s % 2]
        inside = (lanes >= base) & (lanes < base + 8)
        rows[...] = here
        for k in range(8):
            entries[8 * k : 8 * k + 8] = spread(here[:, base + k : base + k + 1])
        e = [[entries[pl.ds(8 * k + i, 8, stride=0), :] if k >= i else None for k in range(8)] for i in range(8)]
        m = [jnp.where(inside, jnp.where(lanes == base + k, 1.0, 0.0), rows[pl.ds(k, 8, stride=0), :]) for k in range(8)]
        end = (s // GROUP + 1) * GROUP
        near = range(s + 1, min(end + AHEAD, 16))
        total = {t: jnp.where(inside, 0.0, strips[t]) for t in near}
        c = {t: [spread(strips[t][:, base + k : base + k + 1]) for k in range(8)] for t in near}
        below = lanes < base + 8
        for k in range(8):
            d = lax.rsqrt(e[k][k])
            u = [e[k][j] * d if j > k else None for j in range(8)]
            for i in range(k + 1, 8):
                for j in range(i, 8):
                    e[i][j] = e[i][j] - u[i] * u[j]
            r = m[k] * d
            for i in range(k + 1, 8):
                m[i] = m[i] - u[i] * r
            for t in near:
                scaled = c[t][k] * d
                for i in range(k + 1, 8):
                    c[t][i] = c[t][i] - u[i] * scaled
                total[t] = total[t] - scaled * r
            inverse_ref[base + k : base + k + 1, :] = jnp.where(below, r, 0.0)[:1]
            row = jnp.where(below, 0.0, r)
            row = jnp.where(lanes == base + k, e[k][k] * d, row)
            for j in range(k + 1, 8):
                row = jnp.where(lanes == base + j, u[j], row)
            upper_ref[base + k : base + k + 1, :] = row[:1]
        for t in near:
            strips[t] = total[t]
        if later:
            later.pop(0)()
        if s + 1 == end and end + AHEAD < 16:
            first, last = 8 * (end - GROUP), 8 * end
            group = lanes[:1] < last
            u_rows = upper_ref[first:last, :]
            delta = block_product(u_rows, jnp.where(group, inverse_ref[first:last, :], u_rows))
            group = (lanes >= first) & (lanes < last)
            for t in range(end + AHEAD, 16):
                strips[t] = jnp.where(group, 0.0, strips[t]) - delta[8 * t : 8 * t + 8]


def cholesky_kernel(column_ref, mine_ref, theirs_ref, out_ref, gram, upper, inverse, rows_ref, entries_ref):
    zero = column_ref[0] == 0
    names = [(0, 0), (0, 1), (1, 1), (0, 2), (0, 3), (2, 2), (2, 3), (3, 3), (1, 2), (1, 3)]
    place = {name: i for i, name in enumerate(names)}
    for i in range(5):
        x, y = mine_ref[i * 128 : i * 128 + 128, :], theirs_ref[i * 128 : i * 128 + 128, :]
        gram[i] = jnp.where(zero, x, y)
        gram[5 + i] = jnp.where(zero, y, x)

    def solve(p, q):
        upper[p * 4 + q] = product(thirds(inverse[p]), thirds(gram[place[p, q]]))

    def update(p, i, j):
        gram[place[i, j]] -= product(thirds(upper[p * 4 + i].T), thirds(upper[p * 4 + j]))

    later = []
    for p in range(4):
        factor_block(gram[place[p, p]], upper.at[p * 4 + p], inverse.at[p], rows_ref, entries_ref, later)
        for work in later:
            work()
        later = []
        for q in range(p):
            upper[p * 4 + q] = jnp.zeros((128, 128), jnp.float32)
        if p < 3:
            solve(p, p + 1)
            update(p, p + 1, p + 1)
        for j in range(p + 2, 4):
            later.append(functools.partial(solve, p, j))
            for i in range(p + 1, j + 1):
                later.append(functools.partial(update, p, i, j))
    for p in range(4):
        for h in range(2):
            out_ref[p * 128 : p * 128 + 128, h * 128 : h * 128 + 128] = jnp.where(zero, upper[p * 4 + h], upper[p * 4 + 2 + h])


def body(design, signs, kept):
    f32 = jnp.float32
    column = lax.axis_index("cols")
    local = pl.pallas_call(
        local_kernel,
        out_shape=jax.ShapeDtypeStruct((2048, 128), f32),
        in_specs=[VMEM, VMEM],
        out_specs=VMEM,
        compiler_params=LIMIT,
        name="local_transform",
    )(design, signs.astype(f32).reshape(8, 128))
    columns = lax.all_to_all(local.reshape(128, 16, 128), ROWS, 0, 0, tiled=True)
    entries = pl.pallas_call(
        functools.partial(select_kernel, 1.0 / math.sqrt(131072)),
        out_shape=jax.ShapeDtypeStruct((1024, 128), f32),
        in_specs=[VMEM, VMEM, pl.BlockSpec(memory_space=pl.ANY)],
        out_specs=VMEM,
        scratch_shapes=[
            pltpu.VMEM((128, 16, 128), f32),
            pltpu.VMEM((64, 128), f32),
            pltpu.VMEM((64, 128), f32),
            pltpu.SMEM((8192,), jnp.int32),
            pltpu.SemaphoreType.DMA(()),
        ],
        compiler_params=LIMIT,
        name="select",
    )(columns, kept.reshape(64, 128), kept)
    entries = lax.all_to_all(entries.reshape(128, 8, 128), ROWS, 0, 0, tiled=True).reshape(1024, 128)
    theirs = swap_cores(entries)
    sketch, blocks = pl.pallas_call(
        functools.partial(own_kernel, 1.0 / 8192),
        out_shape=(jax.ShapeDtypeStruct((64, 256), f32), jax.ShapeDtypeStruct((384, 128), f32)),
        in_specs=[SMEM, VMEM],
        out_specs=(VMEM, VMEM),
        scratch_shapes=[pltpu.VMEM((128, 128), f32)],
        compiler_params=LIMIT,
        cost_estimate=pl.CostEstimate(flops=800_000_000, bytes_accessed=1_000_000, transcendentals=0),
        name="own_gram",
    )(lax.axis_index("rows_0").reshape(1), entries)
    partial = pl.pallas_call(
        functools.partial(cross_kernel, 1.0 / 8192),
        out_shape=jax.ShapeDtypeStruct((640, 128), f32),
        in_specs=[SMEM, VMEM, VMEM, VMEM],
        out_specs=VMEM,
        compiler_params=LIMIT,
        name="cross_gram",
    )(column.reshape(1), entries, theirs, blocks)
    share = jnp.sum(lax.all_to_all(partial.reshape(16, 40, 128), PLANE, 0, 0, tiled=True), axis=0)
    mine = copies(share, PLANE, 16).reshape(640, 128)
    theirs = swap_cores(mine)
    factor = pl.pallas_call(
        cholesky_kernel,
        out_shape=jax.ShapeDtypeStruct((512, 256), f32),
        in_specs=[SMEM, VMEM, VMEM],
        out_specs=VMEM,
        scratch_shapes=[
            pltpu.VMEM((10, 128, 128), f32),
            pltpu.VMEM((16, 128, 128), f32),
            pltpu.VMEM((4, 128, 128), f32),
            pltpu.VMEM((2, 8, 128), f32),
            pltpu.VMEM((2, 64, 128), f32),
        ],
        compiler_params=LIMIT,
        name="cholesky",
    )(column.reshape(1), mine, theirs)
    return sketch, factor


def solution(mesh):
    torus = Mesh(
        mesh.devices.reshape(8, 4, 4, mesh.shape["cols"]), ("rows_0", "rows_1", "rows_2", "cols")
    )
    return jax.shard_map(
        body,
        mesh=torus,
        in_specs=(P(ROWS, "cols"), P(ROWS), P()),
        out_specs=(P(ROWS, "cols"), P(None, "cols")),
        check_vma=False,
    )
```

```python
import functools
import math

import jax
import jax.numpy as jnp
from jax import lax
from jax.experimental import pallas as pl
from jax.experimental.pallas import tpu as pltpu
from jax.sharding import Mesh
from jax.sharding import PartitionSpec as P

ROWS = ("rows_0", "rows_1", "rows_2")
PLANE = ("rows_1", "rows_2")
Z_FASTEST = ("rows_1", "rows_2", "rows_0")
VMEM = pl.BlockSpec(memory_space=pltpu.VMEM)
SMEM = pl.BlockSpec(memory_space=pltpu.SMEM)
LIMIT = pltpu.CompilerParams(vmem_limit_bytes=32 * 1024 * 1024)
WINDOW = 4
GROUP = 2
AHEAD = 2


def butterflies(values):
    values = list(values)
    half = 1
    while half < len(values):
        for low in range(len(values)):
            if not low & half:
                a, b = values[low], values[low | half]
                values[low], values[low | half] = a + b, a - b
        half *= 2
    return values


def sylvester(order):
    parity = lax.broadcasted_iota(jnp.int32, (order, order), 0)
    parity = parity & lax.broadcasted_iota(jnp.int32, (order, order), 1)
    for amount in (4, 2, 1):
        parity = parity ^ (parity >> amount)
    return (1 - 2 * (parity & 1)).astype(jnp.float32).astype(jnp.bfloat16)


def local_kernel(design_ref, signs_ref, out_ref):
    table = sylvester(128)
    for half in range(2):
        parts = []
        for b in range(8):
            piece = design_ref[b * 128 : (b + 1) * 128, half * 128 : (half + 1) * 128].T
            high, middle, low = thirds(piece * signs_ref[b : b + 1, :])
            total = jnp.dot(low, table, preferred_element_type=jnp.float32)
            total += jnp.dot(middle, table, preferred_element_type=jnp.float32)
            total += jnp.dot(high, table, preferred_element_type=jnp.float32)
            parts.append(total)
        for q, mixed in enumerate(butterflies(parts)):
            out_ref[pl.ds(half * 8 + q, 128, stride=16), :] = mixed


def select_kernel(scale, columns_ref, kept_ref, kept_any_ref, out_ref, work, first, second, kept_scalar_ref, sem):
    fetch = pltpu.make_async_copy(kept_any_ref, kept_scalar_ref, sem)
    fetch.start()
    for low in range(16):
        mixed = butterflies(columns_ref[low * 8 + high] for high in range(8))
        for high in range(8):
            work[high * 16 + low] = mixed[high]
    for high in range(8):
        mixed = butterflies(work[high * 16 + low] for low in range(16))
        for low in range(16):
            work[high * 16 + low] = mixed[low]
    fetch.wait()
    sublane = lax.broadcasted_iota(jnp.int32, (8, 128), 0)

    def picked(block, lane, key, so_far):
        found = key == sublane + block * 8
        return tuple(
            jnp.where(found, jnp.take_along_axis(work[block, h * 8 : h * 8 + 8, :], lane, axis=1), so_far[h])
            for h in range(2)
        )

    def ids(chunk):
        wanted = jnp.broadcast_to(kept_ref[pl.ds(chunk, 1), :], (8, 128))
        return wanted & 127, wanted >> 7

    zero = jnp.zeros((8, 128), jnp.float32)

    def merged(values):
        for bit in (1, 2, 4):
            low = (sublane & bit) == 0
            values = [
                jnp.where(low, x, y) + pltpu.roll(jnp.where(low, y, x), 8 - bit, 0)
                for x, y in zip(values[::2], values[1::2])
            ]
        return values[0]

    def group(step, widest):
        sums = [[], []]
        for inner in range(8):
            chunk = step * 8 + inner
            start = kept_scalar_ref[chunk * 128] >> 10
            widest = jnp.maximum(widest, (kept_scalar_ref[chunk * 128 + 127] >> 10) - start)
            lane, key = ids(chunk)
            so_far = (zero, zero)
            for w in range(WINDOW):
                so_far = picked(jnp.minimum(start + w, 127), lane, key, so_far)
            sums[0].append(so_far[0])
            sums[1].append(so_far[1])
        rows = pl.ds(pl.multiple_of(step * 8, 8), 8)
        first[rows, :] = merged(sums[0])
        second[rows, :] = merged(sums[1])
        return widest

    widest = lax.fori_loop(0, 8, group, 0, unroll=True)

    def rest(chunk, carry):
        start = (kept_scalar_ref[chunk * 128] >> 10) + WINDOW
        stop = (kept_scalar_ref[chunk * 128 + 127] >> 10) + 1

        @pl.when(stop > start)
        def _():
            lane, key = ids(chunk)
            more = lax.fori_loop(start, stop, lambda block, c: picked(block, lane, key, c), (zero, zero))
            first[pl.ds(chunk, 1), :] += jnp.sum(more[0], axis=0, keepdims=True)
            second[pl.ds(chunk, 1), :] += jnp.sum(more[1], axis=0, keepdims=True)

        return carry

    @pl.when(widest >= WINDOW)
    def _():
        lax.fori_loop(0, 64, rest, 0)

    left = lax.broadcasted_iota(jnp.int32, (8, 128), 1) < 64
    for h, chosen in enumerate((first, second)):
        for i in range(4):
            x = chosen[16 * i : 16 * i + 8] * scale
            y = chosen[16 * i + 8 : 16 * i + 16] * scale
            even = jnp.where(left, x, pltpu.roll(y, 64, 1))
            odd = jnp.where(left, pltpu.roll(x, 64, 1), y)
            for z in range(8):
                out_ref[pl.ds(z * 8 + h * 4 + i, 8, stride=128), :] = even
                out_ref[pl.ds(64 + z * 8 + h * 4 + i, 8, stride=128), :] = odd


def gram_product(a, b):
    ah, am, al = thirds(a)
    bh, bm, bl = thirds(b)
    top = jnp.concatenate([bh, bm], 1)

    def dot(x, y):
        return lax.dot_general(x, y, (((1,), (1,)), ((), ())), preferred_element_type=jnp.float32)

    small = dot(jnp.concatenate([ah, al], 1), jnp.concatenate([bl, bh], 1))
    small = small + dot(jnp.concatenate([am, am], 1), top)
    return small + dot(jnp.concatenate([ah, ah], 1), top)


def wide(ref, h):
    return jnp.concatenate([ref[pl.ds(h * 4 + i, 128, stride=8), :] for i in range(4)], 1)


def own_kernel(scale, z_ref, mine_ref, sketch_ref, out_ref, turned):
    z = z_ref[0]
    for h in range(2):
        turned[...] = mine_ref[pl.ds(h * 4 + z // 2, 128, stride=8), :].T
        sketch_ref[:, h * 128 : h * 128 + 128] = turned[pl.ds(pl.multiple_of(z % 2 * 64, 64), 64), :]
    both = jnp.concatenate([wide(mine_ref, 0), wide(mine_ref, 1)], 0)
    square = gram_product(both, both) * scale
    for index, block in enumerate([square[:128, :128], square[:128, 128:], square[128:, 128:]]):
        out_ref[index * 128 : (index + 1) * 128, :] = block


def cross_kernel(scale, column_ref, mine_ref, theirs_ref, blocks_ref, out_ref):
    zero = column_ref[0] == 0

    def choose(a, b):
        return jnp.where(zero, a, b)

    own = [wide(mine_ref, 0), wide(mine_ref, 1)]
    other = [wide(theirs_ref, 0), wide(theirs_ref, 1)]
    right = jnp.concatenate([choose(other[0], own[0]), choose(other[1], own[1])], 0)
    cross = gram_product(choose(own[0], other[1]), right) * scale
    out_ref[:384, :] = blocks_ref[...]
    out_ref[384:512, :] = cross[:, :128]
    out_ref[512:, :] = cross[:, 128:]


def copies(shard, axes, count):
    return lax.all_to_all(jnp.broadcast_to(shard[None], (count, *shard.shape)), axes, 0, 0, tiled=True)


def swap_cores(value):
    return lax.ppermute(value, "cols", [(0, 1), (1, 0)])


def thirds(value):
    high = value.astype(jnp.bfloat16)
    rest = value - high.astype(jnp.float32)
    middle = rest.astype(jnp.bfloat16)
    return high, middle, (rest - middle.astype(jnp.float32)).astype(jnp.bfloat16)


def product(left, right):
    (ah, am, al), (bh, bm, bl) = left, right
    top = jnp.concatenate([bh, bm], 0)

    def dot(a, b):
        return lax.dot_general(a, b, (((1,), (0,)), ((), ())), preferred_element_type=jnp.float32)

    small = dot(jnp.concatenate([ah, al], 1), jnp.concatenate([bl, bh], 0))
    small = small + dot(jnp.concatenate([am, am], 1), top)
    return small + dot(jnp.concatenate([ah, ah], 1), top)


def spread(row):
    return jnp.broadcast_to(row, (8, 128))


def block_product(left, right):
    ah, am, al = thirds(left)
    bh, bm, bl = thirds(right)
    return lax.dot_general(
        jnp.concatenate([ah, am, ah, am, al, ah], 0),
        jnp.concatenate([bh, bh, bm, bm, bh, bl], 0),
        (((0,), (0,)), ((), ())),
        preferred_element_type=jnp.float32,
    )


def factor_block(block, upper_ref, inverse_ref, rows_ref, entries_ref, later):
    lanes = lax.broadcasted_iota(jnp.int32, (8, 128), 1)
    strips = [block[8 * s : 8 * s + 8] for s in range(16)]
    for s in range(16):
        here = strips[s]
        base = 8 * s
        rows, entries = rows_ref.at[s % 2], entries_ref.at[s % 2]
        inside = (lanes >= base) & (lanes < base + 8)
        rows[...] = here
        for k in range(8):
            entries[8 * k : 8 * k + 8] = spread(here[:, base + k : base + k + 1])
        e = [[entries[pl.ds(8 * k + i, 8, stride=0), :] if k >= i else None for k in range(8)] for i in range(8)]
        m = [jnp.where(inside, jnp.where(lanes == base + k, 1.0, 0.0), rows[pl.ds(k, 8, stride=0), :]) for k in range(8)]
        end = (s // GROUP + 1) * GROUP
        near = range(s + 1, min(end + AHEAD, 16))
        total = {t: jnp.where(inside, 0.0, strips[t]) for t in near}
        c = {t: [spread(strips[t][:, base + k : base + k + 1]) for k in range(8)] for t in near}
        below = lanes < base + 8
        for k in range(8):
            d = lax.rsqrt(e[k][k])
            u = [e[k][j] * d if j > k else None for j in range(8)]
            for i in range(k + 1, 8):
                for j in range(i, 8):
                    e[i][j] = e[i][j] - u[i] * u[j]
            r = m[k] * d
            for i in range(k + 1, 8):
                m[i] = m[i] - u[i] * r
            for t in near:
                scaled = c[t][k] * d
                for i in range(k + 1, 8):
                    c[t][i] = c[t][i] - u[i] * scaled
                total[t] = total[t] - scaled * r
            inverse_ref[base + k : base + k + 1, :] = jnp.where(below, r, 0.0)[:1]
            row = jnp.where(below, 0.0, r)
            row = jnp.where(lanes == base + k, e[k][k] * d, row)
            for j in range(k + 1, 8):
                row = jnp.where(lanes == base + j, u[j], row)
            upper_ref[base + k : base + k + 1, :] = row[:1]
        for t in near:
            strips[t] = total[t]
        if later:
            later.pop(0)()
        if s + 1 == end and end + AHEAD < 16:
            first, last = 8 * (end - GROUP), 8 * end
            group = lanes[:1] < last
            u_rows = upper_ref[first:last, :]
            delta = block_product(u_rows, jnp.where(group, inverse_ref[first:last, :], u_rows))
            group = (lanes >= first) & (lanes < last)
            for t in range(end + AHEAD, 16):
                strips[t] = jnp.where(group, 0.0, strips[t]) - delta[8 * t : 8 * t + 8]


def cholesky_kernel(column_ref, mine_ref, theirs_ref, out_ref, gram, upper, inverse, rows_ref, entries_ref):
    zero = column_ref[0] == 0
    names = [(0, 0), (0, 1), (1, 1), (0, 2), (0, 3), (2, 2), (2, 3), (3, 3), (1, 2), (1, 3)]
    place = {name: i for i, name in enumerate(names)}
    for i in range(5):
        x, y = mine_ref[i * 128 : i * 128 + 128, :], theirs_ref[i * 128 : i * 128 + 128, :]
        gram[i] = jnp.where(zero, x, y)
        gram[5 + i] = jnp.where(zero, y, x)

    def solve(p, q):
        upper[p * 4 + q] = product(thirds(inverse[p]), thirds(gram[place[p, q]]))

    def update(p, i, j):
        gram[place[i, j]] -= product(thirds(upper[p * 4 + i].T), thirds(upper[p * 4 + j]))

    later = []
    for p in range(4):
        factor_block(gram[place[p, p]], upper.at[p * 4 + p], inverse.at[p], rows_ref, entries_ref, later)
        for work in later:
            work()
        later = []
        for q in range(p):
            upper[p * 4 + q] = jnp.zeros((128, 128), jnp.float32)
        if p < 3:
            solve(p, p + 1)
            update(p, p + 1, p + 1)
        for j in range(p + 2, 4):
            later.append(functools.partial(solve, p, j))
            for i in range(p + 1, j + 1):
                later.append(functools.partial(update, p, i, j))
    for p in range(4):
        for h in range(2):
            out_ref[p * 128 : p * 128 + 128, h * 128 : h * 128 + 128] = jnp.where(zero, upper[p * 4 + h], upper[p * 4 + 2 + h])


def body(design, signs, kept):
    f32 = jnp.float32
    column = lax.axis_index("cols")
    local = pl.pallas_call(
        local_kernel,
        out_shape=jax.ShapeDtypeStruct((2048, 128), f32),
        in_specs=[VMEM, VMEM],
        out_specs=VMEM,
        compiler_params=LIMIT,
        name="local_transform",
    )(design, signs.astype(f32).reshape(8, 128))
    columns = lax.all_to_all(local.reshape(128, 16, 128), Z_FASTEST, 0, 0, tiled=True)
    entries = pl.pallas_call(
        functools.partial(select_kernel, 1.0 / math.sqrt(131072)),
        out_shape=jax.ShapeDtypeStruct((1024, 128), f32),
        in_specs=[VMEM, VMEM, pl.BlockSpec(memory_space=pl.ANY)],
        out_specs=VMEM,
        scratch_shapes=[
            pltpu.VMEM((128, 16, 128), f32),
            pltpu.VMEM((64, 128), f32),
            pltpu.VMEM((64, 128), f32),
            pltpu.SMEM((8192,), jnp.int32),
            pltpu.SemaphoreType.DMA(()),
        ],
        compiler_params=LIMIT,
        name="select",
    )(columns, kept.reshape(64, 128), kept)
    entries = lax.all_to_all(entries.reshape(128, 8, 128), Z_FASTEST, 0, 0, tiled=True).reshape(1024, 128)
    theirs = swap_cores(entries)
    sketch, blocks = pl.pallas_call(
        functools.partial(own_kernel, 1.0 / 8192),
        out_shape=(jax.ShapeDtypeStruct((64, 256), f32), jax.ShapeDtypeStruct((384, 128), f32)),
        in_specs=[SMEM, VMEM],
        out_specs=(VMEM, VMEM),
        scratch_shapes=[pltpu.VMEM((128, 128), f32)],
        compiler_params=LIMIT,
        cost_estimate=pl.CostEstimate(flops=800_000_000, bytes_accessed=1_000_000, transcendentals=0),
        name="own_gram",
    )(lax.axis_index("rows_0").reshape(1), entries)
    partial = pl.pallas_call(
        functools.partial(cross_kernel, 1.0 / 8192),
        out_shape=jax.ShapeDtypeStruct((640, 128), f32),
        in_specs=[SMEM, VMEM, VMEM, VMEM],
        out_specs=VMEM,
        compiler_params=LIMIT,
        name="cross_gram",
    )(column.reshape(1), entries, theirs, blocks)
    share = jnp.sum(lax.all_to_all(partial.reshape(16, 40, 128), PLANE, 0, 0, tiled=True), axis=0)
    mine = copies(share, PLANE, 16).reshape(640, 128)
    theirs = swap_cores(mine)
    factor = pl.pallas_call(
        cholesky_kernel,
        out_shape=jax.ShapeDtypeStruct((512, 256), f32),
        in_specs=[SMEM, VMEM, VMEM],
        out_specs=VMEM,
        scratch_shapes=[
            pltpu.VMEM((10, 128, 128), f32),
            pltpu.VMEM((16, 128, 128), f32),
            pltpu.VMEM((4, 128, 128), f32),
            pltpu.VMEM((2, 8, 128), f32),
            pltpu.VMEM((2, 64, 128), f32),
        ],
        compiler_params=LIMIT,
        name="cholesky",
    )(column.reshape(1), mine, theirs)
    return sketch, factor


def solution(mesh):
    torus = Mesh(
        mesh.devices.reshape(8, 4, 4, mesh.shape["cols"]), ("rows_0", "rows_1", "rows_2", "cols")
    )
    return jax.shard_map(
        body,
        mesh=torus,
        in_specs=(P(ROWS, "cols"), P(ROWS), P()),
        out_specs=(P(ROWS, "cols"), P(None, "cols")),
        check_vma=False,
    )
```

```python
import functools
import math

import jax
import jax.numpy as jnp
from jax import lax
from jax.experimental import pallas as pl
from jax.experimental.pallas import tpu as pltpu
from jax.sharding import Mesh
from jax.sharding import PartitionSpec as P

ROWS = ("rows_0", "rows_1", "rows_2")
PLANE = ("rows_1", "rows_2")
Z_FASTEST = ("rows_1", "rows_2", "rows_0")
VMEM = pl.BlockSpec(memory_space=pltpu.VMEM)
SMEM = pl.BlockSpec(memory_space=pltpu.SMEM)
LIMIT = pltpu.CompilerParams(vmem_limit_bytes=32 * 1024 * 1024)
WINDOW = 4
GROUP = 2
AHEAD = 2


def butterflies(values):
    values = list(values)
    half = 1
    while half < len(values):
        for low in range(len(values)):
            if not low & half:
                a, b = values[low], values[low | half]
                values[low], values[low | half] = a + b, a - b
        half *= 2
    return values


def sylvester(order):
    parity = lax.broadcasted_iota(jnp.int32, (order, order), 0)
    parity = parity & lax.broadcasted_iota(jnp.int32, (order, order), 1)
    for amount in (4, 2, 1):
        parity = parity ^ (parity >> amount)
    return (1 - 2 * (parity & 1)).astype(jnp.float32).astype(jnp.bfloat16)


def local_kernel(design_ref, signs_ref, out_ref):
    table = sylvester(128)
    for half in range(2):
        parts = []
        for b in range(8):
            piece = design_ref[b * 128 : (b + 1) * 128, half * 128 : (half + 1) * 128].T
            high, middle, low = thirds(piece * signs_ref[b : b + 1, :])
            total = jnp.dot(low, table, preferred_element_type=jnp.float32)
            total += jnp.dot(middle, table, preferred_element_type=jnp.float32)
            total += jnp.dot(high, table, preferred_element_type=jnp.float32)
            parts.append(total)
        for q, mixed in enumerate(butterflies(parts)):
            out_ref[pl.ds(half * 8 + q, 128, stride=16), :] = mixed


def select_kernel(scale, columns_ref, kept_ref, kept_any_ref, out_ref, work, first, second, kept_scalar_ref, sem):
    fetch = pltpu.make_async_copy(kept_any_ref, kept_scalar_ref, sem)
    fetch.start()
    for low in range(16):
        mixed = butterflies(columns_ref[low * 8 + high] for high in range(8))
        for high in range(8):
            work[high * 16 + low] = mixed[high]
    for high in range(8):
        mixed = butterflies(work[high * 16 + low] for low in range(16))
        for low in range(16):
            work[high * 16 + low] = mixed[low]
    fetch.wait()
    sublane = lax.broadcasted_iota(jnp.int32, (8, 128), 0)

    def picked(block, lane, key, so_far):
        found = key == sublane + block * 8
        return tuple(
            jnp.where(found, jnp.take_along_axis(work[block, h * 8 : h * 8 + 8, :], lane, axis=1), so_far[h])
            for h in range(2)
        )

    def ids(chunk):
        wanted = jnp.broadcast_to(kept_ref[pl.ds(chunk, 1), :], (8, 128))
        return wanted & 127, wanted >> 7

    zero = jnp.zeros((8, 128), jnp.float32)

    def merged(values):
        for bit in (1, 2, 4):
            low = (sublane & bit) == 0
            values = [
                jnp.where(low, x, y) + pltpu.roll(jnp.where(low, y, x), 8 - bit, 0)
                for x, y in zip(values[::2], values[1::2])
            ]
        return values[0]

    def group(step, widest):
        sums = [[], []]
        for inner in range(8):
            chunk = step * 8 + inner
            start = kept_scalar_ref[chunk * 128] >> 10
            widest = jnp.maximum(widest, (kept_scalar_ref[chunk * 128 + 127] >> 10) - start)
            lane, key = ids(chunk)
            so_far = (zero, zero)
            for w in range(WINDOW):
                so_far = picked(jnp.minimum(start + w, 127), lane, key, so_far)
            sums[0].append(so_far[0])
            sums[1].append(so_far[1])
        rows = pl.ds(pl.multiple_of(step * 8, 8), 8)
        first[rows, :] = merged(sums[0])
        second[rows, :] = merged(sums[1])
        return widest

    widest = lax.fori_loop(0, 8, group, 0, unroll=True)

    def rest(chunk, carry):
        start = (kept_scalar_ref[chunk * 128] >> 10) + WINDOW
        stop = (kept_scalar_ref[chunk * 128 + 127] >> 10) + 1

        @pl.when(stop > start)
        def _():
            lane, key = ids(chunk)
            more = lax.fori_loop(start, stop, lambda block, c: picked(block, lane, key, c), (zero, zero))
            first[pl.ds(chunk, 1), :] += jnp.sum(more[0], axis=0, keepdims=True)
            second[pl.ds(chunk, 1), :] += jnp.sum(more[1], axis=0, keepdims=True)

        return carry

    @pl.when(widest >= WINDOW)
    def _():
        lax.fori_loop(0, 64, rest, 0)

    left = lax.broadcasted_iota(jnp.int32, (8, 128), 1) < 64
    for h, chosen in enumerate((first, second)):
        for i in range(4):
            x = chosen[16 * i : 16 * i + 8] * scale
            y = chosen[16 * i + 8 : 16 * i + 16] * scale
            even = jnp.where(left, x, pltpu.roll(y, 64, 1))
            odd = jnp.where(left, pltpu.roll(x, 64, 1), y)
            for z in range(8):
                out_ref[pl.ds(z * 8 + h * 4 + i, 8, stride=128), :] = even
                out_ref[pl.ds(64 + z * 8 + h * 4 + i, 8, stride=128), :] = odd


def gram_product(a, b):
    ah, am, al = thirds(a)
    bh, bm, bl = thirds(b)
    top = jnp.concatenate([bh, bm], 1)

    def dot(x, y):
        return lax.dot_general(x, y, (((1,), (1,)), ((), ())), preferred_element_type=jnp.float32)

    small = dot(jnp.concatenate([ah, al], 1), jnp.concatenate([bl, bh], 1))
    small = small + dot(jnp.concatenate([am, am], 1), top)
    return small + dot(jnp.concatenate([ah, ah], 1), top)


def wide(ref, h):
    return jnp.concatenate([ref[pl.ds(h * 4 + i, 128, stride=8), :] for i in range(4)], 1)


def own_kernel(scale, z_ref, mine_ref, sketch_ref, out_ref, turned):
    z = z_ref[0]
    for h in range(2):
        turned[...] = mine_ref[pl.ds(h * 4 + z // 2, 128, stride=8), :].T
        sketch_ref[:, h * 128 : h * 128 + 128] = turned[pl.ds(pl.multiple_of(z % 2 * 64, 64), 64), :]
    both = jnp.concatenate([wide(mine_ref, 0), wide(mine_ref, 1)], 0)
    square = gram_product(both, both) * scale
    for index, block in enumerate([square[:128, :128], square[:128, 128:], square[128:, 128:]]):
        out_ref[index * 128 : (index + 1) * 128, :] = block


def cross_kernel(scale, column_ref, mine_ref, theirs_ref, blocks_ref, out_ref):
    zero = column_ref[0] == 0

    def choose(a, b):
        return jnp.where(zero, a, b)

    own = [wide(mine_ref, 0), wide(mine_ref, 1)]
    other = [wide(theirs_ref, 0), wide(theirs_ref, 1)]
    right = jnp.concatenate([choose(other[0], own[0]), choose(other[1], own[1])], 0)
    cross = gram_product(choose(own[0], other[1]), right) * scale
    out_ref[:384, :] = blocks_ref[...]
    out_ref[384:512, :] = cross[:, :128]
    out_ref[512:, :] = cross[:, 128:]


def copies(shard, axes, count):
    return lax.all_to_all(jnp.broadcast_to(shard[None], (count, *shard.shape)), axes, 0, 0, tiled=True)


def swap_cores(value):
    return lax.ppermute(value, "cols", [(0, 1), (1, 0)])


def thirds(value):
    high = value.astype(jnp.bfloat16)
    rest = value - high.astype(jnp.float32)
    middle = rest.astype(jnp.bfloat16)
    return high, middle, (rest - middle.astype(jnp.float32)).astype(jnp.bfloat16)


def product(left, right):
    (ah, am, al), (bh, bm, bl) = left, right
    top = jnp.concatenate([bh, bm], 0)

    def dot(a, b):
        return lax.dot_general(a, b, (((1,), (0,)), ((), ())), preferred_element_type=jnp.float32)

    small = dot(jnp.concatenate([ah, al], 1), jnp.concatenate([bl, bh], 0))
    small = small + dot(jnp.concatenate([am, am], 1), top)
    return small + dot(jnp.concatenate([ah, ah], 1), top)


def spread(row):
    return jnp.broadcast_to(row, (8, 128))


def block_product(left, right):
    ah, am, al = thirds(left)
    bh, bm, bl = thirds(right)
    return lax.dot_general(
        jnp.concatenate([ah, am, ah, am, al, ah], 0),
        jnp.concatenate([bh, bh, bm, bm, bh, bl], 0),
        (((0,), (0,)), ((), ())),
        preferred_element_type=jnp.float32,
    )


def factor_block(block, upper_ref, inverse_ref, rows_ref, entries_ref, later):
    lanes = lax.broadcasted_iota(jnp.int32, (8, 128), 1)
    strips = [block[8 * s : 8 * s + 8] for s in range(16)]
    for s in range(16):
        here = strips[s]
        base = 8 * s
        rows, entries = rows_ref.at[s % 2], entries_ref.at[s % 2]
        inside = (lanes >= base) & (lanes < base + 8)
        rows[...] = here
        for k in range(8):
            entries[8 * k : 8 * k + 8] = spread(here[:, base + k : base + k + 1])
        e = [[entries[pl.ds(8 * k + i, 8, stride=0), :] if k >= i else None for k in range(8)] for i in range(8)]
        m = [jnp.where(inside, jnp.where(lanes == base + k, 1.0, 0.0), rows[pl.ds(k, 8, stride=0), :]) for k in range(8)]
        end = (s // GROUP + 1) * GROUP
        near = range(s + 1, min(end + AHEAD, 16))
        total = {t: jnp.where(inside, 0.0, strips[t]) for t in near}
        c = {t: [spread(strips[t][:, base + k : base + k + 1]) for k in range(8)] for t in near}
        below = lanes < base + 8
        for k in range(8):
            d = lax.rsqrt(e[k][k])
            u = [e[k][j] * d if j > k else None for j in range(8)]
            for i in range(k + 1, 8):
                for j in range(i, 8):
                    e[i][j] = e[i][j] - u[i] * u[j]
            r = m[k] * d
            for i in range(k + 1, 8):
                m[i] = m[i] - u[i] * r
            for t in near:
                scaled = c[t][k] * d
                for i in range(k + 1, 8):
                    c[t][i] = c[t][i] - u[i] * scaled
                total[t] = total[t] - scaled * r
            inverse_ref[base + k : base + k + 1, :] = jnp.where(below, r, 0.0)[:1]
            row = jnp.where(below, 0.0, r)
            row = jnp.where(lanes == base + k, e[k][k] * d, row)
            for j in range(k + 1, 8):
                row = jnp.where(lanes == base + j, u[j], row)
            upper_ref[base + k : base + k + 1, :] = row[:1]
        for t in near:
            strips[t] = total[t]
        if later:
            later.pop(0)()
        if s + 1 == end and end + AHEAD < 16:
            first, last = 8 * (end - GROUP), 8 * end
            group = lanes[:1] < last
            u_rows = upper_ref[first:last, :]
            delta = block_product(u_rows, jnp.where(group, inverse_ref[first:last, :], u_rows))
            group = (lanes >= first) & (lanes < last)
            for t in range(end + AHEAD, 16):
                strips[t] = jnp.where(group, 0.0, strips[t]) - delta[8 * t : 8 * t + 8]


def cholesky_kernel(column_ref, mine_ref, theirs_ref, out_ref, gram, upper, inverse, rows_ref, entries_ref, staged, sems):
    zero = column_ref[0] == 0
    names = [(0, 0), (0, 1), (1, 1), (0, 2), (0, 3), (2, 2), (2, 3), (3, 3), (1, 2), (1, 3)]
    place = {name: i for i, name in enumerate(names)}
    for i in range(5):
        x, y = mine_ref[i * 128 : i * 128 + 128, :], theirs_ref[i * 128 : i * 128 + 128, :]
        gram[i] = jnp.where(zero, x, y)
        gram[5 + i] = jnp.where(zero, y, x)

    def solve(p, q):
        upper[p * 4 + q] = product(thirds(inverse[p]), thirds(gram[place[p, q]]))

    def update(p, i, j):
        gram[place[i, j]] -= product(thirds(upper[p * 4 + i].T), thirds(upper[p * 4 + j]))

    def copy_out(p):
        rows = pl.ds(p * 128, 128)
        return pltpu.make_async_copy(staged.at[rows, :], out_ref.at[rows, :], sems.at[p])

    def send(p):
        for h in range(2):
            staged[p * 128 : p * 128 + 128, h * 128 : h * 128 + 128] = jnp.where(zero, upper[p * 4 + h], upper[p * 4 + 2 + h])
        copy_out(p).start()

    later = []
    for p in range(4):
        factor_block(gram[place[p, p]], upper.at[p * 4 + p], inverse.at[p], rows_ref, entries_ref, later)
        for work in later:
            work()
        later = []
        if p in (1, 2):
            send(p - 1)
        for q in range(p):
            upper[p * 4 + q] = jnp.zeros((128, 128), jnp.float32)
        if p < 3:
            solve(p, p + 1)
            update(p, p + 1, p + 1)
        if p == 2:
            send(2)
        for j in range(p + 2, 4):
            later.append(functools.partial(solve, p, j))
            for i in range(p + 1, j + 1):
                later.append(functools.partial(update, p, i, j))
    send(3)
    for p in range(4):
        copy_out(p).wait()


def body(design, signs, kept):
    f32 = jnp.float32
    column = lax.axis_index("cols")
    local = pl.pallas_call(
        local_kernel,
        out_shape=jax.ShapeDtypeStruct((2048, 128), f32),
        in_specs=[VMEM, VMEM],
        out_specs=VMEM,
        compiler_params=LIMIT,
        name="local_transform",
    )(design, signs.astype(f32).reshape(8, 128))
    columns = lax.all_to_all(local.reshape(128, 16, 128), Z_FASTEST, 0, 0, tiled=True)
    entries = pl.pallas_call(
        functools.partial(select_kernel, 1.0 / math.sqrt(131072)),
        out_shape=jax.ShapeDtypeStruct((1024, 128), f32),
        in_specs=[VMEM, VMEM, pl.BlockSpec(memory_space=pl.ANY)],
        out_specs=VMEM,
        scratch_shapes=[
            pltpu.VMEM((128, 16, 128), f32),
            pltpu.VMEM((64, 128), f32),
            pltpu.VMEM((64, 128), f32),
            pltpu.SMEM((8192,), jnp.int32),
            pltpu.SemaphoreType.DMA(()),
        ],
        compiler_params=LIMIT,
        name="select",
    )(columns, kept.reshape(64, 128), kept)
    entries = lax.all_to_all(entries.reshape(128, 8, 128), Z_FASTEST, 0, 0, tiled=True).reshape(1024, 128)
    theirs = swap_cores(entries)
    sketch, blocks = pl.pallas_call(
        functools.partial(own_kernel, 1.0 / 8192),
        out_shape=(jax.ShapeDtypeStruct((64, 256), f32), jax.ShapeDtypeStruct((384, 128), f32)),
        in_specs=[SMEM, VMEM],
        out_specs=(VMEM, VMEM),
        scratch_shapes=[pltpu.VMEM((128, 128), f32)],
        compiler_params=LIMIT,
        cost_estimate=pl.CostEstimate(flops=800_000_000, bytes_accessed=1_000_000, transcendentals=0),
        name="own_gram",
    )(lax.axis_index("rows_0").reshape(1), entries)
    partial = pl.pallas_call(
        functools.partial(cross_kernel, 1.0 / 8192),
        out_shape=jax.ShapeDtypeStruct((640, 128), f32),
        in_specs=[SMEM, VMEM, VMEM, VMEM],
        out_specs=VMEM,
        compiler_params=LIMIT,
        name="cross_gram",
    )(column.reshape(1), entries, theirs, blocks)
    share = jnp.sum(lax.all_to_all(partial.reshape(16, 40, 128), PLANE, 0, 0, tiled=True), axis=0)
    mine = copies(share, PLANE, 16).reshape(640, 128)
    theirs = swap_cores(mine)
    factor = pl.pallas_call(
        cholesky_kernel,
        out_shape=jax.ShapeDtypeStruct((512, 256), f32),
        in_specs=[SMEM, VMEM, VMEM],
        out_specs=pl.BlockSpec(memory_space=pl.ANY),
        scratch_shapes=[
            pltpu.VMEM((10, 128, 128), f32),
            pltpu.VMEM((16, 128, 128), f32),
            pltpu.VMEM((4, 128, 128), f32),
            pltpu.VMEM((2, 8, 128), f32),
            pltpu.VMEM((2, 64, 128), f32),
            pltpu.VMEM((512, 256), f32),
            pltpu.SemaphoreType.DMA((4,)),
        ],
        compiler_params=LIMIT,
        name="cholesky",
    )(column.reshape(1), mine, theirs)
    return sketch, factor


def solution(mesh):
    torus = Mesh(
        mesh.devices.reshape(8, 4, 4, mesh.shape["cols"]), ("rows_0", "rows_1", "rows_2", "cols")
    )
    return jax.shard_map(
        body,
        mesh=torus,
        in_specs=(P(ROWS, "cols"), P(ROWS), P()),
        out_specs=(P(ROWS, "cols"), P(None, "cols")),
        check_vma=False,
    )
```

```python
import functools
import math

import jax
import jax.numpy as jnp
from jax import lax
from jax.experimental import pallas as pl
from jax.experimental.pallas import tpu as pltpu
from jax.sharding import Mesh
from jax.sharding import PartitionSpec as P

ROWS = ("rows_0", "rows_1", "rows_2")
PLANE = ("rows_1", "rows_2")
Z_FASTEST = ("rows_1", "rows_2", "rows_0")
VMEM = pl.BlockSpec(memory_space=pltpu.VMEM)
SMEM = pl.BlockSpec(memory_space=pltpu.SMEM)
LIMIT = pltpu.CompilerParams(vmem_limit_bytes=32 * 1024 * 1024)
WINDOW = 4
GROUP = 2
AHEAD = 2


def butterflies(values):
    values = list(values)
    half = 1
    while half < len(values):
        for low in range(len(values)):
            if not low & half:
                a, b = values[low], values[low | half]
                values[low], values[low | half] = a + b, a - b
        half *= 2
    return values


def sylvester(order):
    parity = lax.broadcasted_iota(jnp.int32, (order, order), 0)
    parity = parity & lax.broadcasted_iota(jnp.int32, (order, order), 1)
    for amount in (4, 2, 1):
        parity = parity ^ (parity >> amount)
    return (1 - 2 * (parity & 1)).astype(jnp.float32).astype(jnp.bfloat16)


def local_kernel(design_ref, signs_ref, out_ref):
    table = sylvester(128)
    twice = jnp.concatenate([table, table], 0)
    for half in range(2):
        parts = []
        for b in range(8):
            piece = design_ref[b * 128 : (b + 1) * 128, half * 128 : (half + 1) * 128].T
            high, middle, low = thirds(piece * signs_ref[b : b + 1, :])
            total = jnp.dot(low, table, preferred_element_type=jnp.float32)
            total += jnp.dot(jnp.concatenate([high, middle], 1), twice, preferred_element_type=jnp.float32)
            parts.append(total)
        for q, mixed in enumerate(butterflies(parts)):
            out_ref[pl.ds(half * 8 + q, 128, stride=16), :] = mixed


def select_kernel(scale, columns_ref, kept_ref, kept_any_ref, out_ref, work, first, second, kept_scalar_ref, sem):
    fetch = pltpu.make_async_copy(kept_any_ref, kept_scalar_ref, sem)
    fetch.start()
    for low in range(16):
        mixed = butterflies(columns_ref[low * 8 + high] for high in range(8))
        for high in range(8):
            work[high * 16 + low] = mixed[high]
    for high in range(8):
        mixed = butterflies(work[high * 16 + low] for low in range(16))
        for low in range(16):
            work[high * 16 + low] = mixed[low]
    fetch.wait()
    sublane = lax.broadcasted_iota(jnp.int32, (8, 128), 0)

    def picked(block, lane, key, so_far):
        found = key == sublane + block * 8
        return tuple(
            jnp.where(found, jnp.take_along_axis(work[block, h * 8 : h * 8 + 8, :], lane, axis=1), so_far[h])
            for h in range(2)
        )

    def ids(chunk):
        wanted = jnp.broadcast_to(kept_ref[pl.ds(chunk, 1), :], (8, 128))
        return wanted & 127, wanted >> 7

    zero = jnp.zeros((8, 128), jnp.float32)

    def merged(values):
        for bit in (1, 2, 4):
            low = (sublane & bit) == 0
            values = [
                jnp.where(low, x, y) + pltpu.roll(jnp.where(low, y, x), 8 - bit, 0)
                for x, y in zip(values[::2], values[1::2])
            ]
        return values[0]

    def group(step, widest):
        sums = [[], []]
        for inner in range(8):
            chunk = step * 8 + inner
            start = kept_scalar_ref[chunk * 128] >> 10
            widest = jnp.maximum(widest, (kept_scalar_ref[chunk * 128 + 127] >> 10) - start)
            lane, key = ids(chunk)
            so_far = (zero, zero)
            for w in range(WINDOW):
                so_far = picked(jnp.minimum(start + w, 127), lane, key, so_far)
            sums[0].append(so_far[0])
            sums[1].append(so_far[1])
        rows = pl.ds(pl.multiple_of(step * 8, 8), 8)
        first[rows, :] = merged(sums[0])
        second[rows, :] = merged(sums[1])
        return widest

    widest = lax.fori_loop(0, 8, group, 0, unroll=True)

    def rest(chunk, carry):
        start = (kept_scalar_ref[chunk * 128] >> 10) + WINDOW
        stop = (kept_scalar_ref[chunk * 128 + 127] >> 10) + 1

        @pl.when(stop > start)
        def _():
            lane, key = ids(chunk)
            more = lax.fori_loop(start, stop, lambda block, c: picked(block, lane, key, c), (zero, zero))
            first[pl.ds(chunk, 1), :] += jnp.sum(more[0], axis=0, keepdims=True)
            second[pl.ds(chunk, 1), :] += jnp.sum(more[1], axis=0, keepdims=True)

        return carry

    @pl.when(widest >= WINDOW)
    def _():
        lax.fori_loop(0, 64, rest, 0)

    left = lax.broadcasted_iota(jnp.int32, (8, 128), 1) < 64
    for h, chosen in enumerate((first, second)):
        for i in range(4):
            x = chosen[16 * i : 16 * i + 8] * scale
            y = chosen[16 * i + 8 : 16 * i + 16] * scale
            even = jnp.where(left, x, pltpu.roll(y, 64, 1))
            odd = jnp.where(left, pltpu.roll(x, 64, 1), y)
            for z in range(8):
                out_ref[pl.ds(z * 8 + h * 4 + i, 8, stride=128), :] = even
                out_ref[pl.ds(64 + z * 8 + h * 4 + i, 8, stride=128), :] = odd


def gram_product(a, b):
    ah, am, al = thirds(a)
    bh, bm, bl = thirds(b)
    top = jnp.concatenate([bh, bm], 1)

    def dot(x, y):
        return lax.dot_general(x, y, (((1,), (1,)), ((), ())), preferred_element_type=jnp.float32)

    small = dot(jnp.concatenate([ah, al], 1), jnp.concatenate([bl, bh], 1))
    small = small + dot(jnp.concatenate([am, am], 1), top)
    return small + dot(jnp.concatenate([ah, ah], 1), top)


def wide(ref, h):
    return jnp.concatenate([ref[pl.ds(h * 4 + i, 128, stride=8), :] for i in range(4)], 1)


def own_kernel(scale, z_ref, mine_ref, sketch_ref, out_ref, turned):
    z = z_ref[0]
    for h in range(2):
        turned[...] = mine_ref[pl.ds(h * 4 + z // 2, 128, stride=8), :].T
        sketch_ref[:, h * 128 : h * 128 + 128] = turned[pl.ds(pl.multiple_of(z % 2 * 64, 64), 64), :]
    both = jnp.concatenate([wide(mine_ref, 0), wide(mine_ref, 1)], 0)
    square = gram_product(both, both) * scale
    for index, block in enumerate([square[:128, :128], square[:128, 128:], square[128:, 128:]]):
        out_ref[index * 128 : (index + 1) * 128, :] = block


def cross_kernel(scale, column_ref, mine_ref, theirs_ref, blocks_ref, out_ref):
    zero = column_ref[0] == 0

    def choose(a, b):
        return jnp.where(zero, a, b)

    own = [wide(mine_ref, 0), wide(mine_ref, 1)]
    other = [wide(theirs_ref, 0), wide(theirs_ref, 1)]
    right = jnp.concatenate([choose(other[0], own[0]), choose(other[1], own[1])], 0)
    cross = gram_product(choose(own[0], other[1]), right) * scale
    out_ref[:384, :] = blocks_ref[...]
    out_ref[384:512, :] = cross[:, :128]
    out_ref[512:, :] = cross[:, 128:]


def copies(shard, axes, count):
    return lax.all_to_all(jnp.broadcast_to(shard[None], (count, *shard.shape)), axes, 0, 0, tiled=True)


def swap_cores(value):
    return lax.ppermute(value, "cols", [(0, 1), (1, 0)])


def thirds(value):
    high = value.astype(jnp.bfloat16)
    rest = value - high.astype(jnp.float32)
    middle = rest.astype(jnp.bfloat16)
    return high, middle, (rest - middle.astype(jnp.float32)).astype(jnp.bfloat16)


def product(left, right):
    (ah, am, al), (bh, bm, bl) = left, right
    top = jnp.concatenate([bh, bm], 0)

    def dot(a, b):
        return lax.dot_general(a, b, (((1,), (0,)), ((), ())), preferred_element_type=jnp.float32)

    small = dot(jnp.concatenate([ah, al], 1), jnp.concatenate([bl, bh], 0))
    small = small + dot(jnp.concatenate([am, am], 1), top)
    return small + dot(jnp.concatenate([ah, ah], 1), top)


def spread(row):
    return jnp.broadcast_to(row, (8, 128))


def block_product(left, right):
    ah, am, al = thirds(left)
    bh, bm, bl = thirds(right)
    return lax.dot_general(
        jnp.concatenate([ah, am, ah, am, al, ah], 0),
        jnp.concatenate([bh, bh, bm, bm, bh, bl], 0),
        (((0,), (0,)), ((), ())),
        preferred_element_type=jnp.float32,
    )


def factor_block(block, upper_ref, inverse_ref, rows_ref, entries_ref, later):
    lanes = lax.broadcasted_iota(jnp.int32, (8, 128), 1)
    strips = [block[8 * s : 8 * s + 8] for s in range(16)]
    for s in range(16):
        here = strips[s]
        base = 8 * s
        rows, entries = rows_ref.at[s % 2], entries_ref.at[s % 2]
        inside = (lanes >= base) & (lanes < base + 8)
        rows[...] = here
        for k in range(8):
            entries[8 * k : 8 * k + 8] = spread(here[:, base + k : base + k + 1])
        e = [[entries[pl.ds(8 * k + i, 8, stride=0), :] if k >= i else None for k in range(8)] for i in range(8)]
        m = [jnp.where(inside, jnp.where(lanes == base + k, 1.0, 0.0), rows[pl.ds(k, 8, stride=0), :]) for k in range(8)]
        end = (s // GROUP + 1) * GROUP
        near = range(s + 1, min(end + AHEAD, 16))
        total = {t: jnp.where(inside, 0.0, strips[t]) for t in near}
        c = {t: [spread(strips[t][:, base + k : base + k + 1]) for k in range(8)] for t in near}
        below = lanes < base + 8
        for k in range(8):
            d = lax.rsqrt(e[k][k])
            u = [e[k][j] * d if j > k else None for j in range(8)]
            for i in range(k + 1, 8):
                for j in range(i, 8):
                    e[i][j] = e[i][j] - u[i] * u[j]
            r = m[k] * d
            for i in range(k + 1, 8):
                m[i] = m[i] - u[i] * r
            for t in near:
                scaled = c[t][k] * d
                for i in range(k + 1, 8):
                    c[t][i] = c[t][i] - u[i] * scaled
                total[t] = total[t] - scaled * r
            inverse_ref[base + k : base + k + 1, :] = jnp.where(below, r, 0.0)[:1]
            row = jnp.where(below, 0.0, r)
            row = jnp.where(lanes == base + k, e[k][k] * d, row)
            for j in range(k + 1, 8):
                row = jnp.where(lanes == base + j, u[j], row)
            upper_ref[base + k : base + k + 1, :] = row[:1]
        for t in near:
            strips[t] = total[t]
        if later:
            later.pop(0)()
        if s + 1 == end and end + AHEAD < 16:
            first, last = 8 * (end - GROUP), 8 * end
            group = lanes[:1] < last
            u_rows = upper_ref[first:last, :]
            delta = block_product(u_rows, jnp.where(group, inverse_ref[first:last, :], u_rows))
            group = (lanes >= first) & (lanes < last)
            for t in range(end + AHEAD, 16):
                strips[t] = jnp.where(group, 0.0, strips[t]) - delta[8 * t : 8 * t + 8]


def cholesky_kernel(column_ref, mine_ref, theirs_ref, out_ref, gram, upper, inverse, rows_ref, entries_ref, staged, sems):
    zero = column_ref[0] == 0
    names = [(0, 0), (0, 1), (1, 1), (0, 2), (0, 3), (2, 2), (2, 3), (3, 3), (1, 2), (1, 3)]
    place = {name: i for i, name in enumerate(names)}
    for i in range(5):
        x, y = mine_ref[i * 128 : i * 128 + 128, :], theirs_ref[i * 128 : i * 128 + 128, :]
        gram[i] = jnp.where(zero, x, y)
        gram[5 + i] = jnp.where(zero, y, x)

    def solve(p, q):
        upper[p * 4 + q] = product(thirds(inverse[p]), thirds(gram[place[p, q]]))

    def update(p, i, j):
        gram[place[i, j]] -= product(thirds(upper[p * 4 + i].T), thirds(upper[p * 4 + j]))

    def copy_out(p):
        rows = pl.ds(p * 128, 128)
        return pltpu.make_async_copy(staged.at[rows, :], out_ref.at[rows, :], sems.at[p])

    def send(p):
        for h in range(2):
            staged[p * 128 : p * 128 + 128, h * 128 : h * 128 + 128] = jnp.where(zero, upper[p * 4 + h], upper[p * 4 + 2 + h])
        copy_out(p).start()

    later = []
    for p in range(4):
        factor_block(gram[place[p, p]], upper.at[p * 4 + p], inverse.at[p], rows_ref, entries_ref, later)
        for work in later:
            work()
        later = []
        if p in (1, 2):
            send(p - 1)
        for q in range(p):
            upper[p * 4 + q] = jnp.zeros((128, 128), jnp.float32)
        if p < 3:
            solve(p, p + 1)
            update(p, p + 1, p + 1)
        if p == 2:
            send(2)
        for j in range(p + 2, 4):
            later.append(functools.partial(solve, p, j))
            for i in range(p + 1, j + 1):
                later.append(functools.partial(update, p, i, j))
    send(3)
    for p in range(4):
        copy_out(p).wait()


def body(design, signs, kept):
    f32 = jnp.float32
    column = lax.axis_index("cols")
    local = pl.pallas_call(
        local_kernel,
        out_shape=jax.ShapeDtypeStruct((2048, 128), f32),
        in_specs=[VMEM, VMEM],
        out_specs=VMEM,
        compiler_params=LIMIT,
        name="local_transform",
    )(design, signs.astype(f32).reshape(8, 128))
    columns = lax.all_to_all(local.reshape(128, 16, 128), Z_FASTEST, 0, 0, tiled=True)
    entries = pl.pallas_call(
        functools.partial(select_kernel, 1.0 / math.sqrt(131072)),
        out_shape=jax.ShapeDtypeStruct((1024, 128), f32),
        in_specs=[VMEM, VMEM, pl.BlockSpec(memory_space=pl.ANY)],
        out_specs=VMEM,
        scratch_shapes=[
            pltpu.VMEM((128, 16, 128), f32),
            pltpu.VMEM((64, 128), f32),
            pltpu.VMEM((64, 128), f32),
            pltpu.SMEM((8192,), jnp.int32),
            pltpu.SemaphoreType.DMA(()),
        ],
        compiler_params=LIMIT,
        name="select",
    )(columns, kept.reshape(64, 128), kept)
    entries = lax.all_to_all(entries.reshape(128, 8, 128), Z_FASTEST, 0, 0, tiled=True).reshape(1024, 128)
    theirs = swap_cores(entries)
    sketch, blocks = pl.pallas_call(
        functools.partial(own_kernel, 1.0 / 8192),
        out_shape=(jax.ShapeDtypeStruct((64, 256), f32), jax.ShapeDtypeStruct((384, 128), f32)),
        in_specs=[SMEM, VMEM],
        out_specs=(VMEM, VMEM),
        scratch_shapes=[pltpu.VMEM((128, 128), f32)],
        compiler_params=LIMIT,
        cost_estimate=pl.CostEstimate(flops=800_000_000, bytes_accessed=1_000_000, transcendentals=0),
        name="own_gram",
    )(lax.axis_index("rows_0").reshape(1), entries)
    partial = pl.pallas_call(
        functools.partial(cross_kernel, 1.0 / 8192),
        out_shape=jax.ShapeDtypeStruct((640, 128), f32),
        in_specs=[SMEM, VMEM, VMEM, VMEM],
        out_specs=VMEM,
        compiler_params=LIMIT,
        name="cross_gram",
    )(column.reshape(1), entries, theirs, blocks)
    share = jnp.sum(lax.all_to_all(partial.reshape(16, 40, 128), PLANE, 0, 0, tiled=True), axis=0)
    mine = copies(share, PLANE, 16).reshape(640, 128)
    theirs = swap_cores(mine)
    factor = pl.pallas_call(
        cholesky_kernel,
        out_shape=jax.ShapeDtypeStruct((512, 256), f32),
        in_specs=[SMEM, VMEM, VMEM],
        out_specs=pl.BlockSpec(memory_space=pl.ANY),
        scratch_shapes=[
            pltpu.VMEM((10, 128, 128), f32),
            pltpu.VMEM((16, 128, 128), f32),
            pltpu.VMEM((4, 128, 128), f32),
            pltpu.VMEM((2, 8, 128), f32),
            pltpu.VMEM((2, 64, 128), f32),
            pltpu.VMEM((512, 256), f32),
            pltpu.SemaphoreType.DMA((4,)),
        ],
        compiler_params=LIMIT,
        name="cholesky",
    )(column.reshape(1), mine, theirs)
    return sketch, factor


def solution(mesh):
    torus = Mesh(
        mesh.devices.reshape(8, 4, 4, mesh.shape["cols"]), ("rows_0", "rows_1", "rows_2", "cols")
    )
    return jax.shard_map(
        body,
        mesh=torus,
        in_specs=(P(ROWS, "cols"), P(ROWS), P()),
        out_specs=(P(ROWS, "cols"), P(None, "cols")),
        check_vma=False,
    )
```
